32 devices in a mesh: chan: 16 (over z, x, core), pix: 2 (over y).
Axes of the slice: x: 2, y: 2, z: 4, core: 2. Of those that a mesh axis runs over, the one named last changes fastest.
Arguments:
- cube: float32 [512, 16384], P('pix', 'chan'), as said below
- windows: int32 [8], replicated, may hold values from 1 to 1024, as said below
- mask: int32 [16384], replicated, may hold values from 0 to 1, as said below
Outputs:
- subtracted: float32 [512, 16384], P('pix', 'chan')
The draws below stay inside these ranges and needn't reach their ends.
Inputs may be any that keep to these rules, and one draw needn't show every extreme that they name: windows[0] is 1024 and windows[7] is 1; for 0 < k < 7, windows[k] is at most 1024 halved k times (rounded down) and more than three quarters of that, but 1 or more. `mask`: zero on 8 disjoint ranges of 256 to 512 channels each, one elsewhere; the k-th range lies inside channels k * 2048 to (k + 1) * 2048 - 1, at least 512 channels from that slot's edges, and at least 1024 channels from either end of the band. `cube`: each spectrum is a smooth continuum of low order plus noise whose level varies from channel to channel.
All inputs are finite; a program needn't handle non-finite values.
Results may differ from the reference program's by a relative error of at most 0.00021.
Values sent between devices are 32-bit elements; how exact they have to be, the bound alone decides.
A program may use at most 64 MiB of HBM per device.

```python
import jax
import jax.numpy as jnp
from jax import lax

NC = 16384
TERMS = 16
PASSES = 8
WMAX = 1024
PIX_DEV = 16
NPIX = 512


def draw_cube(key, part):
    keys = jax.random.split(key, 4)
    xvals = (2.0 * jnp.arange(NC).astype(jnp.float32) + 1.0) / NC - 1.0
    table = jnp.stack([jnp.ones_like(xvals), xvals, 1.5 * xvals * xvals - 0.5, 2.5 * xvals ** 3 - 1.5 * xvals], axis=0)
    level = jax.random.uniform(keys[0], (NPIX, 1), jnp.float32, 3.0, 10.0)
    slopes = jax.random.normal(keys[1], (NPIX, 3), jnp.float32)
    coefs = jnp.concatenate([level, slopes], axis=1)
    continuum = coefs @ table
    chan_scale = jnp.exp(jax.random.uniform(keys[2], (1, NC), jnp.float32, jnp.log(0.5), jnp.log(2.0)))
    noise = jax.random.normal(keys[3], (NPIX, NC), jnp.float32)
    return (continuum + noise * chan_scale).astype(jnp.float32)


def draw_windows(key, part):
    steps = jnp.arange(PASSES, dtype=jnp.int32)
    base = jnp.right_shift(jnp.int32(WMAX), steps)
    spread = jnp.maximum(1, jnp.right_shift(jnp.int32(WMAX), steps + 2))
    jitter = jax.random.randint(key, (PASSES,), 0, spread, jnp.int32)
    widths = jnp.maximum(1, base - jitter)
    widths = widths.at[0].set(WMAX)
    widths = widths.at[PASSES - 1].set(1)
    return widths.astype(jnp.int32)


def draw_mask(key, part):
    keys = jax.random.split(key, 2)
    slot = NC // 8
    slots = jnp.arange(8, dtype=jnp.int32)[:, None]
    spans = jax.random.randint(keys[0], (8, 1), NC // 64, NC // 32 + 1, jnp.int32)
    low_margin = jnp.where(slots == 0, NC // 16, NC // 32).astype(jnp.int32)
    high_margin = jnp.where(slots == 7, NC // 16, NC // 32).astype(jnp.int32)
    room = slot - low_margin - high_margin - spans + 1
    offsets = jax.random.randint(keys[1], (8, 1), 0, 1 << 20, jnp.int32) % room
    starts = slots * slot + low_margin + offsets
    column = jnp.arange(NC, dtype=jnp.int32)[None, :]
    inside = (column >= starts) & (column < starts + spans)
    return (1 - jnp.any(inside, axis=0).astype(jnp.int32)).astype(jnp.int32)


def setup_inputs(seed: int = 0) -> dict:
    key_list = jax.random.split(jax.random.key(seed), 4)
    cube = draw_cube(jax.random.fold_in(key_list[3], 71), 0)
    windows = draw_windows(jax.random.fold_in(key_list[3], 71), 0)
    mask = draw_mask(jax.random.fold_in(key_list[3], 71), 0)
    return {"cube": cube, "windows": windows, "mask": mask}


def legendre(xvals):
    rows = [jnp.ones_like(xvals), xvals]
    for order in range(1, TERMS - 1):
        rows.append(((2.0 * order + 1.0) * xvals * rows[order] - order * rows[order - 1]) / (order + 1.0))
    return jnp.stack(rows[:TERMS], axis=0)

def snip(spectra, windows):
    count = spectra.shape[1]
    column = lax.broadcasted_iota(jnp.int32, (1, count), 1)
    for step in range(PASSES):
        width = windows[step]
        padded = jnp.pad(spectra, ((0, 0), (WMAX, WMAX)))
        lower = lax.dynamic_slice_in_dim(padded, (WMAX - width).astype(jnp.int32), count, 1)
        upper = lax.dynamic_slice_in_dim(padded, (WMAX + width).astype(jnp.int32), count, 1)
        inside = (column >= width) & (column < count - width)
        spectra = jnp.where(inside, jnp.minimum(spectra, 0.5 * (lower + upper)), spectra)
    return spectra

def reference(cube, windows, mask):
    xvals = (2.0 * jnp.arange(NC, dtype=jnp.int32).astype(jnp.float32) + 1.0) / NC - 1.0
    table = legendre(xvals)
    weighted = table * mask.astype(jnp.float32)[None, :]
    gram = jnp.dot(weighted, table.T, precision=lax.Precision.HIGHEST)
    factor = jnp.linalg.cholesky(gram)

    def one_block(block):
        baseline = snip(block, windows)
        rhs = jnp.dot(weighted, baseline.T, precision=lax.Precision.HIGHEST)
        middle = lax.linalg.triangular_solve(factor, rhs, left_side=True, lower=True)
        coef = lax.linalg.triangular_solve(factor, middle, left_side=True, lower=True, transpose_a=True)
        return block - jnp.dot(coef.T, table, precision=lax.Precision.HIGHEST)
    blocks = cube.reshape(NPIX // PIX_DEV, PIX_DEV, NC)
    return lax.map(one_block, blocks).reshape(NPIX, NC)
```

```python
import functools
import math

import jax
import jax.numpy as jnp
import numpy as np
from jax import lax
from jax.experimental import pallas as pl
from jax.experimental.pallas import tpu as pltpu
from jax.sharding import PartitionSpec as P

TERMS = 16
PASSES = 8
WMAX = 1024
HALO = 2 * WMAX
LANES = 128
CHUNKS = 8
LAG = 4
SPLIT = 4
MESH = pl.DeviceIdType.MESH
F32 = jnp.float32
BF16 = jnp.bfloat16


def chunk_spans(rows):
    part = max(8, rows // CHUNKS)
    return [(start, part) for start in range(0, rows, part)]


def linearization():
    def a(r):
        return math.comb(2 * r, r) / 2.0**r

    out = np.zeros((2 * TERMS - 1, TERMS, TERMS))
    for n in range(TERMS):
        for m in range(TERMS):
            for r in range(min(n, m) + 1):
                k = n + m - 2 * r
                out[k, n, m] = (
                    a(r) * a(n - r) * a(m - r) / a(n + m - r)
                    * (2 * k + 1) / (2 * n + 2 * m - 2 * r + 1)
                )
    return out.astype(np.float32)


def next_legendre(order, xvals, here, before):
    return ((2.0 * order + 1.0) * xvals * here - order * before) * (1.0 / (order + 1.0))


def split3(v):
    hi = v.astype(BF16)
    rest = v - hi.astype(F32)
    mid = rest.astype(BF16)
    lo = (rest - mid.astype(F32)).astype(BF16)
    return hi, mid, lo


def kernel(
    n_chan, group, total,
    windows_hbm, cube, mask_sq_hbm, mask_row_hbm, lin_hbm,
    left_out, right_out, mine,
    windows, mask_sq, mask_row, lin, raw, ping, pong, fit, table, w3, sums,
    load_sem, mine_sem, token, own_sem, send_sem, hop_sem, recv_sem, up_sem, down_sem, sum_send, sum_recv,
):
    pix, ch = cube.shape
    rows = raw.shape[0]
    slab_ch = group * ch
    tiles = slab_ch // LANES
    slabs = n_chan // group
    spans = chunk_spans(rows)
    me = lax.axis_index("chan")
    slab = me // group
    g = lax.rem(me, group)
    own_col = pl.multiple_of(HALO + g * ch, LANES)

    def peer(b):
        return {"chan": slab * group + b}

    own_rows = pl.multiple_of(g * rows, 8)
    barrier = pltpu.get_barrier_semaphore()

    def greet(device):
        pl.semaphore_signal(
            barrier, inc=1, device_id={"chan": device}, device_id_type=MESH
        )

    for k in range(1, group):
        greet(slab * group + lax.rem(g + k, group))

    @pl.when(slab > 0)
    def _():
        greet(me - group)

    @pl.when(slab < slabs - 1)
    def _():
        greet(me + group)

    loads = [
        pltpu.make_async_copy(mask_sq_hbm, mask_sq, load_sem.at[0]),
        pltpu.make_async_copy(mask_row_hbm, mask_row, load_sem.at[1]),
        pltpu.make_async_copy(lin_hbm, lin, load_sem.at[2]),
        pltpu.make_async_copy(windows_hbm, windows, load_sem.at[3]),
    ]
    own = pltpu.make_async_copy(
        cube.at[pl.ds(own_rows, rows), :], raw.at[:, pl.ds(own_col, ch)], own_sem
    )
    kept = pltpu.make_async_copy(cube, mine, mine_sem)
    for copy in loads:
        copy.start()
    own.start()

    @pl.when(slab == 0)
    def _():
        raw[:, 0:HALO] = jnp.full((rows, HALO), jnp.inf, F32)

    @pl.when(slab == slabs - 1)
    def _():
        raw[:, HALO + slab_ch :] = jnp.full((rows, HALO), jnp.inf, F32)

    near = group - 1 + jnp.where(slab > 0, 1, 0) + jnp.where(slab < slabs - 1, 1, 0)
    pl.semaphore_wait(barrier, near)

    points = min(slabs, 3)

    def relay(point):
        for up in (True, False):
            place = slab if up else slabs - 1 - slab
            sem = token.at[0 if up else 1]
            to = me + group if up else me - group
            turn = (place == point) if point < points - 1 else (place >= point)

            @pl.when(turn)
            def _():
                if point > 0:
                    pl.semaphore_wait(sem, 1)

                @pl.when(place < slabs - 1)
                def _():
                    pl.semaphore_signal(
                        sem, inc=1, device_id={"chan": to}, device_id_type=MESH
                    )

    def chunk(c):
        return pl.ds(*spans[c])

    def slab_send(c, b):
        return pltpu.make_async_remote_copy(
            src_ref=cube.at[pl.ds(b * rows + spans[c][0], spans[c][1]), :],
            dst_ref=raw.at[chunk(c), pl.ds(own_col, ch)],
            send_sem=send_sem, recv_sem=recv_sem.at[c, g],
            device_id=peer(b), device_id_type=MESH,
        )

    def slab_recv(c, b):
        return pltpu.make_async_remote_copy(
            src_ref=cube.at[chunk(c), :],
            dst_ref=raw.at[chunk(c), pl.ds(HALO + b * ch, ch)],
            send_sem=send_sem, recv_sem=recv_sem.at[c, b],
            device_id=peer(b), device_id_type=MESH,
        )

    def hop(c, b, up, from_own):
        if up:
            col = b * ch - (slab_ch - HALO)
            sem, to = up_sem.at[c], me + group
        else:
            col = HALO + slab_ch + b * ch
            sem, to = down_sem.at[c], me - group
        if from_own:
            src = cube.at[pl.ds(pl.multiple_of(own_rows + spans[c][0], 8), spans[c][1]), :]
        else:
            src = raw.at[chunk(c), pl.ds(HALO + b * ch, ch)]
        return pltpu.make_async_remote_copy(
            src_ref=src, dst_ref=raw.at[chunk(c), pl.ds(col, ch)],
            send_sem=hop_sem.at[0 if up else 1], recv_sem=sem,
            device_id={"chan": to}, device_id_type=MESH,
        )

    def goes_up(b):
        return b * ch >= slab_ch - HALO

    def goes_down(b):
        return b * ch < HALO

    def own_hops(c):
        for b in range(group):
            if goes_up(b):
                @pl.when((g == b) & (slab < slabs - 1))
                def _():
                    hop(c, b, True, True).start()
            if goes_down(b):
                @pl.when((g == b) & (slab > 0))
                def _():
                    hop(c, b, False, True).start()

    def pass_on(c, b):
        slab_recv(c, b).wait_recv()
        if goes_up(b):
            @pl.when(slab < slabs - 1)
            def _():
                hop(c, b, True, False).start()
        if goes_down(b):
            @pl.when(slab > 0)
            def _():
                hop(c, b, False, False).start()

    def forward(c, near):
        for b in range(group):
            @pl.when((g != b) & ((g // 2 == b // 2) == near))
            def _():
                pass_on(c, b)

    def halo_wait(c):
        def arrived(col, sem):
            return pltpu.make_async_remote_copy(
                src_ref=raw.at[chunk(c), pl.ds(col, HALO)],
                dst_ref=raw.at[chunk(c), pl.ds(col, HALO)],
                send_sem=hop_sem.at[0], recv_sem=sem,
                device_id={"chan": me}, device_id_type=MESH,
            )

        @pl.when(slab > 0)
        def _():
            arrived(0, up_sem.at[c]).wait_recv()

        @pl.when(slab < slabs - 1)
        def _():
            arrived(HALO + slab_ch, down_sem.at[c]).wait_recv()

    for c in range(len(spans)):
        for b in range(group):
            @pl.when(g != b)
            def _():
                slab_send(c, b).start()
        own_hops(c)
    kept.start()
    relay(0)
    for copy in loads:
        copy.wait()

    shape = mask_sq.shape
    index = lax.broadcasted_iota(jnp.int32, shape, 0) * shape[1] + lax.broadcasted_iota(
        jnp.int32, shape, 1
    )
    xvals = (2.0 * index.astype(F32) + 1.0) * (1.0 / total) - 1.0
    keep = mask_sq[...].astype(F32)
    here, before = jnp.ones_like(xvals), jnp.zeros_like(xvals)
    gram = jnp.zeros((TERMS, TERMS), F32)
    for k in range(2 * TERMS - 1):
        moment = jnp.sum(here * keep, axis=0, keepdims=True)
        moment = jnp.sum(moment, axis=1, keepdims=True)
        gram = gram + moment * lin[k]
        here, before = next_legendre(k, xvals, here, before), here

    row_id = lax.broadcasted_iota(jnp.int32, (TERMS, 2 * TERMS), 0)
    col_id = lax.broadcasted_iota(jnp.int32, (TERMS, 2 * TERMS), 1)
    eye = jnp.where(row_id + TERMS == col_id, 1.0, 0.0).astype(F32)
    aug = eye + jnp.concatenate([gram, jnp.zeros_like(gram)], axis=1)
    for p in range(TERMS):
        lead = aug[p : p + 1, :] / aug[p : p + 1, p : p + 1]
        aug = jnp.where(row_id == p, lead, aug - aug[:, p : p + 1] * lead)
    inverse = aug[:, TERMS:]

    step = min(1024, slab_ch)
    base = slab * slab_ch
    for s in range(0, slab_ch, step):
        lane = lax.broadcasted_iota(jnp.int32, (1, step), 1)
        x_s = (2.0 * (base + s + lane).astype(F32) + 1.0) * (1.0 / total) - 1.0
        here, before = jnp.ones_like(x_s), jnp.zeros_like(x_s)
        for n in range(TERMS):
            table[n : n + 1, s : s + step] = here
            here, before = next_legendre(n, x_s, here, before), here
        keep_s = mask_row[:, pl.ds(pl.multiple_of(base + s, LANES), step)].astype(F32)
        hi, mid, lo = split3(table[:, s : s + step] * keep_s)
        w3[0:TERMS, s : s + step] = hi
        w3[TERMS : 2 * TERMS, s : s + step] = mid
        w3[2 * TERMS :, s : s + step] = lo

    for c in range(len(spans)):
        forward(c, True)

    own.wait()
    edge = HALO // LANES

    def snip(start, block):
        r = pl.ds(start, block)
        lane = lax.broadcasted_iota(jnp.int32, (block, LANES), 1)

        def at(ref, t):
            return ref[0:block, (t + edge) * LANES : (t + edge + 1) * LANES]

        def put(ref, t, v):
            ref[0:block, (t + edge) * LANES : (t + edge + 1) * LANES] = v

        def first(t):
            return raw[r, (t + edge) * LANES : (t + edge + 1) * LANES]

        far = WMAX // LANES
        for t in range(-far, tiles + far):
            put(ping, t, jnp.minimum(first(t), 0.5 * (first(t - far) + first(t + far))))
        src, dst = ping, pong
        for k in range(1, PASSES):
            bound = max(LANES, WMAX >> k)
            b = bound // LANES
            d = bound - windows[k]
            back = lax.rem(LANES - d, LANES)
            low_here = lane < LANES - d
            high_here = lane >= d
            reach = 0 if k == PASSES - 1 else b
            left = {}
            right = {}
            for t in range(-reach, tiles + reach):
                for u in (t - b, t - b + 1):
                    if u not in left:
                        left[u] = pltpu.roll(at(src, u), back, 1)
                for u in (t + b - 1, t + b):
                    if u not in right:
                        right[u] = pltpu.roll(at(src, u), d, 1)
                lower = jnp.where(low_here, left[t - b], left[t - b + 1])
                upper = jnp.where(high_here, right[t + b], right[t + b - 1])
                v = jnp.minimum(at(src, t), 0.5 * (lower + upper))
                if k < PASSES - 1:
                    put(dst, t, v)
                else:
                    cols = slice(t * LANES, (t + 1) * LANES)
                    fit[r, cols] = v
            src, dst = dst, src

    def process(c):
        halo_wait(c)
        snip(*spans[c])

    dims = (((1,), (1,)), ((), ()))

    def products(lo, hi):
        whole = fit[lo:hi, :]
        fit_hi = whole.astype(BF16)
        fit_lo = (whole - fit_hi.astype(F32)).astype(BF16)
        rhs3 = lax.dot_general(w3[...], fit_hi, dims, preferred_element_type=F32)
        rhs3 = rhs3 + lax.dot_general(w3[...], fit_lo, dims, preferred_element_type=F32)
        return rhs3[0:TERMS] + (rhs3[TERMS : 2 * TERMS] + rhs3[2 * TERMS :])

    count = len(spans)
    lag = min(LAG, count)
    cut = spans[-1][0] - spans[-1][1]
    for c in range(count + lag):
        if c < count:
            forward(c, False)
        if c >= lag:
            process(c - lag)
            if c - lag < points - 1:
                relay(c - lag + 1)
            if c - lag == count - 3:
                early = products(0, cut)
    rhs = jnp.concatenate([early, products(cut, rows)], axis=1)
    fold = sums.shape[2] // rows
    high = TERMS // fold
    packed = jnp.concatenate([rhs[i * high : (i + 1) * high] for i in range(fold)], axis=1)
    sums[me] = packed

    def sum_copy(k):
        return pltpu.make_async_remote_copy(
            src_ref=sums.at[me], dst_ref=sums.at[me],
            send_sem=sum_send, recv_sem=sum_recv,
            device_id={"chan": lax.rem(me + k, n_chan)}, device_id_type=MESH,
        )

    for k in range(1, n_chan):
        sum_copy(k).start()

    t_own = table[:, pl.ds(pl.multiple_of(g * ch, LANES), ch)]
    shaped = jnp.zeros_like(t_own)
    for m in range(TERMS):
        shaped = shaped + inverse[:, m : m + 1] * t_own[m : m + 1, :]
    a_hi, a_mid, a_lo = split3(shaped)
    zero = jnp.zeros_like(a_hi)
    right_out[...] = jnp.concatenate(
        [a_hi, a_mid, a_hi, a_lo, a_hi, a_mid, zero, zero], axis=0
    )

    def sent(ref, sem):
        return pltpu.make_async_remote_copy(
            src_ref=ref, dst_ref=ref, send_sem=sem, recv_sem=own_sem,
            device_id={"chan": me}, device_id_type=MESH,
        )

    if group > 1:
        sent(cube.at[0 : (group - 1) * rows, :], send_sem).wait_send()

    @pl.when(slab < slabs - 1)
    def _():
        sent(raw.at[:, 0:HALO], hop_sem.at[0]).wait_send()

    @pl.when(slab > 0)
    def _():
        sent(raw.at[:, 0:HALO], hop_sem.at[1]).wait_send()

    others = sums.at[0 : n_chan - 1]
    everyone = pltpu.make_async_remote_copy(
        src_ref=others, dst_ref=others, send_sem=sum_send, recv_sem=sum_recv,
        device_id={"chan": me}, device_id_type=MESH,
    )
    everyone.wait_send()
    everyone.wait_recv()
    kept.wait()

    for b in range(group):
        tot = sums[b]
        for z in range(1, slabs):
            tot = tot + sums[z * group + b]
        tot = jnp.concatenate(
            [tot[:, i * rows : (i + 1) * rows] for i in range(fold)], axis=0
        )
        hi, mid, lo = (v.astype(F32) for v in split3(tot))
        none = jnp.zeros_like(hi)
        left_side = jnp.concatenate([hi, hi, mid, hi, lo, mid, none, none], axis=0)
        left_out[b * rows : (b + 1) * rows, :] = left_side.T.astype(BF16)


def subtract(cube, left, right, out, buf, sem):
    step = max(cube.shape[0] // SPLIT, 16)
    for start in range(0, cube.shape[0], step):
        r = pl.ds(start, step)
        buf[r, :] = cube[r, :] - jnp.dot(left[r, :], right[...], preferred_element_type=F32)
        pltpu.make_async_copy(buf.at[r, :], out.at[r, :], sem).start()
    pltpu.make_async_copy(buf, out, sem).wait()


def per_device(cube, windows, mask):
    pix, ch = cube.shape
    n_chan = lax.axis_size("chan")
    total = ch * n_chan
    group = min(n_chan, max(4, HALO // ch))
    slab_ch = group * ch
    rows = pix // group
    wide = slab_ch + 2 * HALO
    fold = max(1, LANES // rows)
    vmem = pl.BlockSpec(memory_space=pltpu.VMEM)
    hbm = pl.BlockSpec(memory_space=pl.ANY)
    dma = pltpu.SemaphoreType.DMA
    chunks = len(chunk_spans(rows))
    part = rows // chunks
    lin = jnp.asarray(linearization())
    depth = 8 * TERMS
    kept = pl.pallas_call(
        functools.partial(kernel, n_chan, group, total),
        out_shape=(
            pltpu.VMEM((pix, depth), BF16),
            pltpu.VMEM((depth, ch), BF16),
            pltpu.VMEM((pix, ch), F32),
        ),
        in_specs=[hbm, hbm, hbm, hbm, hbm],
        out_specs=(vmem, vmem, vmem),
        scratch_shapes=[
            pltpu.SMEM(windows.shape, jnp.int32),
            pltpu.VMEM((total // LANES, LANES), jnp.int32),
            pltpu.VMEM((1, total), jnp.int32),
            pltpu.VMEM(lin.shape, F32),
            pltpu.VMEM((rows, wide), F32),
            pltpu.VMEM((part, wide), F32),
            pltpu.VMEM((part, wide), F32),
            pltpu.VMEM((rows, slab_ch), F32),
            pltpu.VMEM((TERMS, slab_ch), F32),
            pltpu.VMEM((3 * TERMS, slab_ch), BF16),
            pltpu.VMEM((n_chan, TERMS // fold, rows * fold), F32),
            dma((4,)), dma, pltpu.SemaphoreType.REGULAR((2,)), dma, dma, dma((2,)),
            dma((chunks, group)), dma((chunks,)), dma((chunks,)),
            dma, dma,
        ],
        compiler_params=pltpu.CompilerParams(
            collective_id=0, has_side_effects=True
        ),
    )(windows, cube, mask.reshape(-1, LANES), mask.reshape(1, total), lin)
    left, right, mine = (pltpu.with_memory_space_constraint(a, pltpu.VMEM) for a in kept)
    return pl.pallas_call(
        subtract,
        out_shape=jax.ShapeDtypeStruct((pix, ch), F32),
        in_specs=[vmem, vmem, vmem],
        out_specs=hbm,
        scratch_shapes=[pltpu.VMEM((pix, ch), F32), dma],
    )(mine, left, right)


def solution(mesh):
    placed = (P("pix", "chan"), P(), P())
    return jax.shard_map(
        per_device, mesh=mesh, in_specs=placed, out_specs=P("pix", "chan"), check_vma=False
    )
```

```python
import functools
import math

import jax
import jax.numpy as jnp
import numpy as np
from jax import lax
from jax.experimental import pallas as pl
from jax.experimental.pallas import tpu as pltpu
from jax.sharding import PartitionSpec as P

TERMS = 16
PASSES = 8
WMAX = 1024
HALO = 2 * WMAX
LANES = 128
CHUNKS = 8
LAG = 3
AHEAD = 3
SPLIT = 4
MESH = pl.DeviceIdType.MESH
F32 = jnp.float32
BF16 = jnp.bfloat16


def chunk_spans(rows):
    part = max(8, rows // CHUNKS)
    return [(start, part) for start in range(0, rows, part)]


def linearization():
    def a(r):
        return math.comb(2 * r, r) / 2.0**r

    out = np.zeros((2 * TERMS - 1, TERMS, TERMS))
    for n in range(TERMS):
        for m in range(TERMS):
            for r in range(min(n, m) + 1):
                k = n + m - 2 * r
                out[k, n, m] = (
                    a(r) * a(n - r) * a(m - r) / a(n + m - r)
                    * (2 * k + 1) / (2 * n + 2 * m - 2 * r + 1)
                )
    return out.astype(np.float32)


def next_legendre(order, xvals, here, before):
    return ((2.0 * order + 1.0) * xvals * here - order * before) * (1.0 / (order + 1.0))


def split3(v):
    hi = v.astype(BF16)
    rest = v - hi.astype(F32)
    mid = rest.astype(BF16)
    lo = (rest - mid.astype(F32)).astype(BF16)
    return hi, mid, lo


def kernel(
    n_chan, group, total,
    windows_hbm, cube, mask_sq_hbm, mask_row_hbm, lin_hbm,
    left_out, right_out, mine,
    windows, mask_sq, mask_row, lin, raw, ping, pong, fit, table, w3, sums,
    load_sem, own_sem, token, send_sem, near_sem, far_sem, halo_sem, sum_send, sum_recv,
):
    pix, ch = cube.shape
    rows = raw.shape[0]
    slab_ch = group * ch
    tiles = slab_ch // LANES
    slabs = n_chan // group
    spans = chunk_spans(rows)
    me = lax.axis_index("chan")
    slab = me // group
    g = lax.rem(me, group)
    own_col = pl.multiple_of(HALO + g * ch, LANES)

    def peer(b):
        return {"chan": slab * group + b}

    own_rows = pl.multiple_of(g * rows, 8)
    barrier = pltpu.get_barrier_semaphore()

    def greet(device):
        pl.semaphore_signal(
            barrier, inc=1, device_id={"chan": device}, device_id_type=MESH
        )

    for k in range(1, group):
        greet(slab * group + lax.rem(g + k, group))

    @pl.when(slab > 0)
    def _():
        greet(me - group)

    @pl.when(slab < slabs - 1)
    def _():
        greet(me + group)

    loads = [
        pltpu.make_async_copy(mask_sq_hbm, mask_sq, load_sem.at[0]),
        pltpu.make_async_copy(mask_row_hbm, mask_row, load_sem.at[1]),
        pltpu.make_async_copy(lin_hbm, lin, load_sem.at[2]),
        pltpu.make_async_copy(windows_hbm, windows, load_sem.at[3]),
    ]
    own = pltpu.make_async_copy(
        cube.at[pl.ds(own_rows, rows), :], raw.at[:, pl.ds(own_col, ch)], own_sem
    )
    kept = pltpu.make_async_copy(cube, mine, own_sem)
    for copy in loads:
        copy.start()
    own.start()

    @pl.when(slab == 0)
    def _():
        raw[:, 0:HALO] = jnp.full((rows, HALO), jnp.inf, F32)

    @pl.when(slab == slabs - 1)
    def _():
        raw[:, HALO + slab_ch :] = jnp.full((rows, HALO), jnp.inf, F32)

    near = group - 1 + jnp.where(slab > 0, 1, 0) + jnp.where(slab < slabs - 1, 1, 0)
    pl.semaphore_wait(barrier, near)

    points = min(slabs, len(spans))

    def relay(point):
        for up in (True, False):
            place = slab if up else slabs - 1 - slab
            sem = token.at[0 if up else 1]
            to = me + group if up else me - group
            turn = (place == point) if point < points - 1 else (place >= point)

            @pl.when(turn)
            def _():
                if point > 0:
                    pl.semaphore_wait(sem, 1)

                @pl.when(place < slabs - 1)
                def _():
                    pl.semaphore_signal(
                        sem, inc=1, device_id={"chan": to}, device_id_type=MESH
                    )

    def chunk(c):
        return pl.ds(*spans[c])

    def remote(src, dst, recv_sem, to):
        return pltpu.make_async_remote_copy(
            src_ref=src, dst_ref=dst, send_sem=send_sem, recv_sem=recv_sem,
            device_id=to, device_id_type=MESH,
        )

    def near_send(b):
        return remote(
            cube.at[b * rows : (b + 1) * rows, :], raw.at[:, pl.ds(own_col, ch)], near_sem, peer(b)
        )

    def far_send(c, b):
        return remote(
            cube.at[pl.ds(b * rows + spans[c][0], spans[c][1]), :],
            raw.at[chunk(c), pl.ds(own_col, ch)], far_sem.at[c], peer(b),
        )

    def hop(c, b, up, from_own):
        col = b * ch - (slab_ch - HALO) if up else HALO + slab_ch + b * ch
        if from_own:
            src = cube.at[pl.ds(pl.multiple_of(own_rows + spans[c][0], 8), spans[c][1]), :]
        else:
            src = raw.at[chunk(c), pl.ds(HALO + b * ch, ch)]
        to = {"chan": me + group if up else me - group}
        return remote(src, raw.at[chunk(c), pl.ds(col, ch)], halo_sem.at[c], to)

    def amount(r, width, recv_sem):
        ref = raw.at[r, 0:width]
        return remote(ref, ref, recv_sem, {"chan": me})

    inner = (slab > 0) & (slab < slabs - 1)

    def sided(wait):
        if slabs > 1:
            pl.when(inner)(lambda: wait(2 * HALO))
            pl.when(jnp.logical_not(inner))(lambda: wait(HALO))
        else:
            wait(0)

    def goes_up(b):
        return b * ch >= slab_ch - HALO

    def goes_down(b):
        return b * ch < HALO

    def own_hops(c):
        for b in range(group):
            if goes_up(b):
                @pl.when((g == b) & (slab < slabs - 1))
                def _():
                    hop(c, b, True, True).start()
            if goes_down(b):
                @pl.when((g == b) & (slab > 0))
                def _():
                    hop(c, b, False, True).start()

    def pass_on(c, b):
        if goes_up(b):
            @pl.when(slab < slabs - 1)
            def _():
                hop(c, b, True, False).start()
        if goes_down(b):
            @pl.when(slab > 0)
            def _():
                hop(c, b, False, False).start()

    def forward_near():
        amount(pl.ds(0, rows), ch, near_sem).wait_recv()
        for c in range(len(spans)):
            if c >= AHEAD:
                own_hops(c)
            for b in range(group):
                @pl.when((g != b) & (g // 2 == b // 2))
                def _():
                    pass_on(c, b)

    def forward_far(c):
        amount(chunk(c), (group - 2) * ch, far_sem.at[c]).wait_recv()
        for b in range(group):
            @pl.when(g // 2 != b // 2)
            def _():
                pass_on(c, b)

    def halo_wait(c):
        if slabs > 1:
            sided(lambda width: amount(chunk(c), width, halo_sem.at[c]).wait_recv())

    for c in range(len(spans)):
        for b in range(group):
            @pl.when(g // 2 != b // 2)
            def _():
                far_send(c, b).start()
        if c == 0:
            for b in range(group):
                @pl.when((g != b) & (g // 2 == b // 2))
                def _():
                    near_send(b).start()
        if c < AHEAD:
            own_hops(c)
    relay(0)
    for copy in loads:
        copy.wait()

    shape = mask_sq.shape
    index = lax.broadcasted_iota(jnp.int32, shape, 0) * shape[1] + lax.broadcasted_iota(
        jnp.int32, shape, 1
    )
    xvals = (2.0 * index.astype(F32) + 1.0) * (1.0 / total) - 1.0
    keep = mask_sq[...].astype(F32)
    here, before = jnp.ones_like(xvals), jnp.zeros_like(xvals)
    gram = jnp.zeros((TERMS, TERMS), F32)
    for k in range(2 * TERMS - 1):
        moment = jnp.sum(here * keep, axis=0, keepdims=True)
        moment = jnp.sum(moment, axis=1, keepdims=True)
        gram = gram + moment * lin[k]
        here, before = next_legendre(k, xvals, here, before), here

    row_id = lax.broadcasted_iota(jnp.int32, (TERMS, 2 * TERMS), 0)
    col_id = lax.broadcasted_iota(jnp.int32, (TERMS, 2 * TERMS), 1)
    eye = jnp.where(row_id + TERMS == col_id, 1.0, 0.0).astype(F32)
    aug = eye + jnp.concatenate([gram, jnp.zeros_like(gram)], axis=1)
    for p in range(TERMS):
        lead = aug[p : p + 1, :] / aug[p : p + 1, p : p + 1]
        aug = jnp.where(row_id == p, lead, aug - aug[:, p : p + 1] * lead)
    inverse = aug[:, TERMS:]

    half = slab_ch // 2
    step = min(1024, half)
    base = slab * slab_ch

    def weigh(q):
        parts = []
        for s in (q * step, half + q * step):
            lane = lax.broadcasted_iota(jnp.int32, (1, step), 1)
            x_s = (2.0 * (base + s + lane).astype(F32) + 1.0) * (1.0 / total) - 1.0
            here, before = jnp.ones_like(x_s), jnp.zeros_like(x_s)
            for n in range(TERMS):
                table[n : n + 1, s : s + step] = here
                here, before = next_legendre(n, x_s, here, before), here
            keep_s = mask_row[:, pl.ds(pl.multiple_of(base + s, LANES), step)].astype(F32)
            parts += [v.astype(F32) for v in split3(table[:, s : s + step] * keep_s)]
        parts.append(jnp.zeros((2 * TERMS, step), F32))
        w3[q * step : (q + 1) * step, :] = jnp.concatenate(parts, axis=0).T.astype(BF16)

    def shape_own():
        t_own = table[:, pl.ds(pl.multiple_of(g * ch, LANES), ch)]
        shaped = jnp.zeros_like(t_own)
        for m in range(TERMS):
            shaped = shaped + inverse[:, m : m + 1] * t_own[m : m + 1, :]
        a_hi, a_mid, a_lo = split3(shaped)
        zero = jnp.zeros_like(a_hi)
        right_out[...] = jnp.concatenate(
            [a_hi, a_mid, a_hi, a_lo, a_hi, a_mid, zero, zero], axis=0
        )

    forward_near()
    kept.start()
    if points > 1:
        relay(1)
    edge = HALO // LANES

    def snip(start, block):
        r = pl.ds(start, block)
        lane = lax.broadcasted_iota(jnp.int32, (block, LANES), 1)

        def at(ref, t):
            return ref[0:block, (t + edge) * LANES : (t + edge + 1) * LANES]

        def put(ref, t, v):
            ref[0:block, (t + edge) * LANES : (t + edge + 1) * LANES] = v

        def first(t):
            return raw[r, (t + edge) * LANES : (t + edge + 1) * LANES]

        far = WMAX // LANES
        for t in range(-far, tiles + far):
            put(ping, t, jnp.minimum(first(t), 0.5 * (first(t - far) + first(t + far))))
        src, dst = ping, pong
        for k in range(1, PASSES):
            bound = max(LANES, WMAX >> k)
            b = bound // LANES
            d = bound - windows[k]
            back = lax.rem(LANES - d, LANES)
            low_here = lane < LANES - d
            high_here = lane >= d
            reach = 0 if k == PASSES - 1 else b
            left = {}
            right = {}
            for t in range(-reach, tiles + reach):
                for u in (t - b, t - b + 1):
                    if u not in left:
                        left[u] = pltpu.roll(at(src, u), back, 1)
                for u in (t + b - 1, t + b):
                    if u not in right:
                        right[u] = pltpu.roll(at(src, u), d, 1)
                lower = jnp.where(low_here, left[t - b], left[t - b + 1])
                upper = jnp.where(high_here, right[t + b], right[t + b - 1])
                v = jnp.minimum(at(src, t), 0.5 * (lower + upper))
                if k < PASSES - 1:
                    put(dst, t, v)
                else:
                    cols = slice(t * LANES, (t + 1) * LANES)
                    fit[r, cols] = v
            src, dst = dst, src

    def process(c):
        halo_wait(c)
        snip(*spans[c])

    part = spans[0][1]
    lanes = lax.broadcasted_iota(jnp.int32, (part, LANES), 1)
    place = lanes // TERMS

    def gather(v):
        for shift in (4 * TERMS, 2 * TERMS, TERMS):
            v = v + pltpu.roll(v, shift, 1)
        return v

    def products(c):
        whole = fit[chunk(c), :]
        hi = whole.astype(BF16).astype(F32)
        lo = whole - hi
        both = jnp.concatenate(
            [hi[:, 0:half], lo[:, 0:half], hi[:, half:], lo[:, half:]], axis=0
        ).astype(BF16)
        rhs = jnp.dot(both, w3[...], preferred_element_type=F32)
        low = rhs[0:part] + rhs[part : 2 * part]
        high = rhs[2 * part : 3 * part] + rhs[3 * part :]
        return jnp.where(lanes < 3 * TERMS, low, high)

    def send_sums(late):
        mine_at = sums.at[late * n_chan + me]
        for k in range(1, n_chan):
            pltpu.make_async_remote_copy(
                src_ref=mine_at, dst_ref=mine_at,
                send_sem=sum_send, recv_sem=sum_recv.at[late],
                device_id={"chan": lax.rem(me + k, n_chan)}, device_id_type=MESH,
            ).start()

    count = len(spans)
    lag = min(LAG, count)
    pairs = half // step
    early = jnp.zeros((part, LANES), F32)
    filled = raw.at[:, 0 : (group + 1) * ch]
    for c in range(count + lag):
        if c < count:
            forward_far(c)
        if c < lag:
            for q in range(c * pairs // lag, (c + 1) * pairs // lag):
                weigh(q)
            if c == lag - 1:
                shape_own()
        if 2 <= c + 1 < points:
            relay(c + 1)
        if c == lag:
            pltpu.make_async_copy(filled, filled, own_sem).wait()
        if c >= lag:
            done = c - lag
            process(done)
            found = products(done)
            if done < count - 1:
                early = jnp.where(place == done, gather(found), early)
            if done == count - 2:
                sums[me] = early
                send_sums(0)
    sums[n_chan + me] = found
    send_sums(1)

    sided(lambda width: amount(pl.ds(0, rows), (group - 1) * ch + width, near_sem).wait_send())

    def sums_wait(first, blocks, recv):
        ref = sums.at[first : first + blocks]
        return pltpu.make_async_remote_copy(
            src_ref=ref, dst_ref=ref, send_sem=sum_send, recv_sem=recv,
            device_id={"chan": me}, device_id_type=MESH,
        )

    def put_left(start, spread):
        spread = gather(spread)
        hi, mid, lo = (v.astype(F32) for v in split3(spread))
        spot = lax.broadcasted_iota(jnp.int32, spread.shape, 1) // TERMS
        picked = jnp.where(spot == 4, lo, jnp.zeros_like(lo))
        picked = jnp.where((spot == 2) | (spot == 5), mid, picked)
        picked = jnp.where((spot < 2) | (spot == 3), hi, picked)
        left_out[start : start + spread.shape[0], :] = picked.astype(BF16)

    def over_slabs(late, b):
        tot = sums[late * n_chan + b]
        for z in range(1, slabs):
            tot = tot + sums[late * n_chan + z * group + b]
        return tot

    sums_wait(0, n_chan - 1, sum_recv.at[0]).wait_recv()
    for b in range(group):
        tot = over_slabs(0, b)
        put_left(
            b * rows,
            jnp.concatenate([jnp.where(place == c, tot, 0.0) for c in range(count - 1)], axis=0),
        )
    sums_wait(0, 2 * (n_chan - 1), sum_recv.at[0]).wait_send()
    sums_wait(0, n_chan - 1, sum_recv.at[1]).wait_recv()
    for b in range(group):
        put_left(b * rows + spans[-1][0], over_slabs(1, b))


def subtract(cube, left, right, out, buf, sem):
    step = max(cube.shape[0] // SPLIT, 16)
    for start in range(0, cube.shape[0], step):
        r = pl.ds(start, step)
        buf[r, :] = cube[r, :] - jnp.dot(left[r, :], right[...], preferred_element_type=F32)
        pltpu.make_async_copy(buf.at[r, :], out.at[r, :], sem).start()
    pltpu.make_async_copy(buf, out, sem).wait()


def per_device(cube, windows, mask):
    pix, ch = cube.shape
    n_chan = lax.axis_size("chan")
    total = ch * n_chan
    group = min(n_chan, max(4, HALO // ch))
    slab_ch = group * ch
    rows = pix // group
    wide = slab_ch + 2 * HALO
    vmem = pl.BlockSpec(memory_space=pltpu.VMEM)
    hbm = pl.BlockSpec(memory_space=pl.ANY)
    dma = pltpu.SemaphoreType.DMA
    chunks = len(chunk_spans(rows))
    part = rows // chunks
    lin = jnp.asarray(linearization())
    depth = 8 * TERMS
    kept = pl.pallas_call(
        functools.partial(kernel, n_chan, group, total),
        out_shape=(
            pltpu.VMEM((pix, depth), BF16),
            pltpu.VMEM((depth, ch), BF16),
            pltpu.VMEM((pix, ch), F32),
        ),
        in_specs=[hbm, hbm, hbm, hbm, hbm],
        out_specs=(vmem, vmem, vmem),
        scratch_shapes=[
            pltpu.SMEM(windows.shape, jnp.int32),
            pltpu.VMEM((total // LANES, LANES), jnp.int32),
            pltpu.VMEM((1, total), jnp.int32),
            pltpu.VMEM(lin.shape, F32),
            pltpu.VMEM((rows, wide), F32),
            pltpu.VMEM((part, wide), F32),
            pltpu.VMEM((part, wide), F32),
            pltpu.VMEM((rows, slab_ch), F32),
            pltpu.VMEM((TERMS, slab_ch), F32),
            pltpu.VMEM((slab_ch // 2, LANES), BF16),
            pltpu.VMEM((2 * n_chan, part, LANES), F32),
            dma((4,)), dma, pltpu.SemaphoreType.REGULAR((2,)), dma, dma,
            dma((chunks,)), dma((chunks,)), dma, dma((2,)),
        ],
        compiler_params=pltpu.CompilerParams(
            collective_id=0, has_side_effects=True
        ),
    )(windows, cube, mask.reshape(-1, LANES), mask.reshape(1, total), lin)
    left, right, mine = (pltpu.with_memory_space_constraint(a, pltpu.VMEM) for a in kept)
    return pl.pallas_call(
        subtract,
        out_shape=jax.ShapeDtypeStruct((pix, ch), F32),
        in_specs=[vmem, vmem, vmem],
        out_specs=hbm,
        scratch_shapes=[pltpu.VMEM((pix, ch), F32), dma],
    )(mine, left, right)


def solution(mesh):
    placed = (P("pix", "chan"), P(), P())
    return jax.shard_map(
        per_device, mesh=mesh, in_specs=placed, out_specs=P("pix", "chan"), check_vma=False
    )
```

```python
import functools
import math

import jax
import jax.numpy as jnp
import numpy as np
from jax import lax
from jax.experimental import pallas as pl
from jax.experimental.pallas import tpu as pltpu
from jax.sharding import PartitionSpec as P

TERMS = 16
PASSES = 8
WMAX = 1024
HALO = 2 * WMAX
LANES = 128
CHUNKS = 8
LAG = 3
AHEAD = 3
PIECES = 2
WINDOW = 10
MESH = pl.DeviceIdType.MESH
F32 = jnp.float32
BF16 = jnp.bfloat16


def chunk_spans(rows):
    part = max(8, rows // CHUNKS)
    return [(start, part) for start in range(0, rows, part)]


def linearization():
    def a(r):
        return math.comb(2 * r, r) / 2.0**r

    out = np.zeros((2 * TERMS - 1, TERMS, TERMS))
    for n in range(TERMS):
        for m in range(TERMS):
            for r in range(min(n, m) + 1):
                k = n + m - 2 * r
                out[k, n, m] = (
                    a(r) * a(n - r) * a(m - r) / a(n + m - r)
                    * (2 * k + 1) / (2 * n + 2 * m - 2 * r + 1)
                )
    return out.astype(np.float32)


def next_legendre(order, xvals, here, before):
    return ((2.0 * order + 1.0) * xvals * here - order * before) * (1.0 / (order + 1.0))


def split3(v):
    hi = v.astype(BF16)
    rest = v - hi.astype(F32)
    mid = rest.astype(BF16)
    lo = (rest - mid.astype(F32)).astype(BF16)
    return hi, mid, lo


def kernel(
    n_chan, group, total,
    windows_hbm, cube, mask_sq_hbm, mask_row_hbm, lin_hbm,
    left_out, right_out, mine,
    windows, mask_sq, mask_row, lin, raw, ping, pong, fit, table, w3, sums,
    load_sem, own_sem, token, send_sem, near_sem, far_sem, halo_sem, sum_send, sum_recv,
):
    pix, ch = cube.shape
    rows = raw.shape[0]
    slab_ch = group * ch
    tiles = slab_ch // LANES
    slabs = n_chan // group
    spans = chunk_spans(rows)
    pieces = far_sem.shape[1]
    bit = ch // pieces
    me = lax.axis_index("chan")
    slab = me // group
    g = lax.rem(me, group)
    own_col = pl.multiple_of(HALO + g * ch, LANES)

    def peer(b):
        return {"chan": slab * group + b}

    own_rows = pl.multiple_of(g * rows, 8)
    barrier = pltpu.get_barrier_semaphore()

    def greet(device):
        pl.semaphore_signal(
            barrier, inc=1, device_id={"chan": device}, device_id_type=MESH
        )

    for k in range(1, group):
        greet(slab * group + lax.rem(g + k, group))

    @pl.when(slab > 0)
    def _():
        greet(me - group)

    @pl.when(slab < slabs - 1)
    def _():
        greet(me + group)

    loads = [
        pltpu.make_async_copy(mask_sq_hbm, mask_sq, load_sem.at[0]),
        pltpu.make_async_copy(mask_row_hbm, mask_row, load_sem.at[1]),
        pltpu.make_async_copy(lin_hbm, lin, load_sem.at[2]),
        pltpu.make_async_copy(windows_hbm, windows, load_sem.at[3]),
    ]
    own = pltpu.make_async_copy(
        cube.at[pl.ds(own_rows, rows), :], raw.at[:, pl.ds(own_col, ch)], own_sem
    )
    kept = pltpu.make_async_copy(cube, mine, own_sem)
    for copy in loads:
        copy.start()
    own.start()

    @pl.when(slab == 0)
    def _():
        raw[:, 0:HALO] = jnp.full((rows, HALO), jnp.inf, F32)

    @pl.when(slab == slabs - 1)
    def _():
        raw[:, HALO + slab_ch :] = jnp.full((rows, HALO), jnp.inf, F32)

    near = group - 1 + jnp.where(slab > 0, 1, 0) + jnp.where(slab < slabs - 1, 1, 0)
    pl.semaphore_wait(barrier, near)

    points = min(slabs, len(spans))

    def relay(point):
        for up in (True, False):
            place = slab if up else slabs - 1 - slab
            sem = token.at[0 if up else 1]
            to = me + group if up else me - group
            turn = (place == point) if point < points - 1 else (place >= point)

            @pl.when(turn)
            def _():
                if point > 0:
                    pl.semaphore_wait(sem, 1)

                @pl.when(place < slabs - 1)
                def _():
                    pl.semaphore_signal(
                        sem, inc=1, device_id={"chan": to}, device_id_type=MESH
                    )

    def chunk(c):
        return pl.ds(*spans[c])

    def remote(src, dst, recv_sem, to):
        return pltpu.make_async_remote_copy(
            src_ref=src, dst_ref=dst, send_sem=send_sem, recv_sem=recv_sem,
            device_id=to, device_id_type=MESH,
        )

    def near_send(b):
        return remote(
            cube.at[b * rows : (b + 1) * rows, :], raw.at[:, pl.ds(own_col, ch)], near_sem, peer(b)
        )

    def far_send(c, p, b):
        return remote(
            cube.at[pl.ds(b * rows + spans[c][0], spans[c][1]), pl.ds(p * bit, bit)],
            raw.at[chunk(c), pl.ds(pl.multiple_of(own_col + p * bit, LANES), bit)],
            far_sem.at[c, p], peer(b),
        )

    def hop(c, b, up, from_own, first=0, width=None):
        width = ch if width is None else width
        col = first + (b * ch - (slab_ch - HALO) if up else HALO + slab_ch + b * ch)
        if from_own:
            src = cube.at[pl.ds(pl.multiple_of(own_rows + spans[c][0], 8), spans[c][1]), :]
        else:
            src = raw.at[chunk(c), pl.ds(HALO + b * ch + first, width)]
        to = {"chan": me + group if up else me - group}
        return remote(src, raw.at[chunk(c), pl.ds(col, width)], halo_sem.at[c], to)

    def amount(r, width, recv_sem):
        ref = raw.at[r, 0:width]
        return remote(ref, ref, recv_sem, {"chan": me})

    inner = (slab > 0) & (slab < slabs - 1)

    def sided(wait):
        if slabs > 1:
            pl.when(inner)(lambda: wait(2 * HALO))
            pl.when(jnp.logical_not(inner))(lambda: wait(HALO))
        else:
            wait(0)

    def goes_up(b):
        return b * ch >= slab_ch - HALO

    def goes_down(b):
        return b * ch < HALO

    def own_hops(c):
        for b in range(group):
            if goes_up(b):
                @pl.when((g == b) & (slab < slabs - 1))
                def _():
                    hop(c, b, True, True).start()
            if goes_down(b):
                @pl.when((g == b) & (slab > 0))
                def _():
                    hop(c, b, False, True).start()

    def pass_on(c, b, *stretch):
        if goes_up(b):
            @pl.when(slab < slabs - 1)
            def _():
                hop(c, b, True, False, *stretch).start()
        if goes_down(b):
            @pl.when(slab > 0)
            def _():
                hop(c, b, False, False, *stretch).start()

    def forward_near():
        amount(pl.ds(0, rows), ch, near_sem).wait_recv()
        for c in range(len(spans)):
            if c >= AHEAD:
                own_hops(c)
            for b in range(group):
                @pl.when((g != b) & (g // 2 == b // 2))
                def _():
                    pass_on(c, b)

    def feed(c, p):
        for b in range(group):
            @pl.when(g // 2 != b // 2)
            def _():
                far_send(c, p, b).start()

    def forward_far(c, p):
        amount(chunk(c), (group - 2) * bit, far_sem.at[c, p]).wait_recv()
        for b in range(group):
            @pl.when(g // 2 != b // 2)
            def _():
                pass_on(c, b, p * bit, bit)
        later = c * pieces + p + WINDOW
        if later < len(spans) * pieces:
            feed(later // pieces, later % pieces)

    def halo_wait(c):
        if slabs > 1:
            sided(lambda width: amount(chunk(c), width, halo_sem.at[c]).wait_recv())

    for c in range(len(spans)):
        for p in range(pieces):
            if c * pieces + p < WINDOW:
                feed(c, p)
        if c == 0:
            for b in range(group):
                @pl.when((g != b) & (g // 2 == b // 2))
                def _():
                    near_send(b).start()
        if c < AHEAD:
            own_hops(c)
    relay(0)
    for copy in loads:
        copy.wait()

    shape = mask_sq.shape
    index = lax.broadcasted_iota(jnp.int32, shape, 0) * shape[1] + lax.broadcasted_iota(
        jnp.int32, shape, 1
    )
    xvals = (2.0 * index.astype(F32) + 1.0) * (1.0 / total) - 1.0
    keep = mask_sq[...].astype(F32)
    here, before = jnp.ones_like(xvals), jnp.zeros_like(xvals)
    gram = jnp.zeros((TERMS, TERMS), F32)
    for k in range(2 * TERMS - 1):
        moment = jnp.sum(here * keep, axis=0, keepdims=True)
        moment = jnp.sum(moment, axis=1, keepdims=True)
        gram = gram + moment * lin[k]
        here, before = next_legendre(k, xvals, here, before), here

    row_id = lax.broadcasted_iota(jnp.int32, (TERMS, 2 * TERMS), 0)
    col_id = lax.broadcasted_iota(jnp.int32, (TERMS, 2 * TERMS), 1)
    eye = jnp.where(row_id + TERMS == col_id, 1.0, 0.0).astype(F32)
    aug = eye + jnp.concatenate([gram, jnp.zeros_like(gram)], axis=1)
    for p in range(TERMS):
        lead = aug[p : p + 1, :] / aug[p : p + 1, p : p + 1]
        aug = jnp.where(row_id == p, lead, aug - aug[:, p : p + 1] * lead)
    inverse = aug[:, TERMS:]

    half = slab_ch // 2
    step = min(1024, half)
    base = slab * slab_ch

    def weigh(q):
        parts = []
        for s in (q * step, half + q * step):
            lane = lax.broadcasted_iota(jnp.int32, (1, step), 1)
            x_s = (2.0 * (base + s + lane).astype(F32) + 1.0) * (1.0 / total) - 1.0
            here, before = jnp.ones_like(x_s), jnp.zeros_like(x_s)
            for n in range(TERMS):
                table[n : n + 1, s : s + step] = here
                here, before = next_legendre(n, x_s, here, before), here
            keep_s = mask_row[:, pl.ds(pl.multiple_of(base + s, LANES), step)].astype(F32)
            parts += [v.astype(F32) for v in split3(table[:, s : s + step] * keep_s)]
        parts.append(jnp.zeros((2 * TERMS, step), F32))
        w3[q * step : (q + 1) * step, :] = jnp.concatenate(parts, axis=0).T.astype(BF16)

    def shape_own():
        t_own = table[:, pl.ds(pl.multiple_of(g * ch, LANES), ch)]
        shaped = jnp.zeros_like(t_own)
        for m in range(TERMS):
            shaped = shaped + inverse[:, m : m + 1] * t_own[m : m + 1, :]
        a_hi, a_mid, a_lo = split3(shaped)
        zero = jnp.zeros_like(a_hi)
        right_out[...] = jnp.concatenate(
            [a_hi, a_mid, a_hi, a_lo, a_hi, a_mid, zero, zero], axis=0
        )

    forward_near()
    kept.start()
    if points > 1:
        relay(1)
    edge = HALO // LANES

    def snip(start, block):
        r = pl.ds(start, block)
        lane = lax.broadcasted_iota(jnp.int32, (block, LANES), 1)

        def at(ref, t):
            return ref[0:block, (t + edge) * LANES : (t + edge + 1) * LANES]

        def put(ref, t, v):
            ref[0:block, (t + edge) * LANES : (t + edge + 1) * LANES] = v

        def first(t):
            return raw[r, (t + edge) * LANES : (t + edge + 1) * LANES]

        far = WMAX // LANES
        for t in range(-far, tiles + far):
            put(ping, t, jnp.minimum(first(t), 0.5 * (first(t - far) + first(t + far))))
        src, dst = ping, pong
        for k in range(1, PASSES):
            bound = max(LANES, WMAX >> k)
            b = bound // LANES
            d = bound - windows[k]
            back = lax.rem(LANES - d, LANES)
            low_here = lane < LANES - d
            high_here = lane >= d
            reach = 0 if k == PASSES - 1 else b
            left = {}
            right = {}
            for t in range(-reach, tiles + reach):
                for u in (t - b, t - b + 1):
                    if u not in left:
                        left[u] = pltpu.roll(at(src, u), back, 1)
                for u in (t + b - 1, t + b):
                    if u not in right:
                        right[u] = pltpu.roll(at(src, u), d, 1)
                lower = jnp.where(low_here, left[t - b], left[t - b + 1])
                upper = jnp.where(high_here, right[t + b], right[t + b - 1])
                v = jnp.minimum(at(src, t), 0.5 * (lower + upper))
                if k < PASSES - 1:
                    put(dst, t, v)
                else:
                    cols = slice(t * LANES, (t + 1) * LANES)
                    fit[r, cols] = v
            src, dst = dst, src

    def process(c):
        halo_wait(c)
        snip(*spans[c])

    part = spans[0][1]
    place = lax.broadcasted_iota(jnp.int32, (part, LANES), 1) // TERMS

    def gather(v):
        for shift in (4 * TERMS, 2 * TERMS, TERMS):
            v = v + pltpu.roll(v, shift, 1)
        return v

    def products(first, last):
        tall = (last - first + 1) * part
        whole = fit[spans[first][0] : spans[first][0] + tall, :]
        hi = whole.astype(BF16).astype(F32)
        lo = whole - hi
        both = jnp.concatenate(
            [hi[:, 0:half], lo[:, 0:half], hi[:, half:], lo[:, half:]], axis=0
        ).astype(BF16)
        rhs = jnp.dot(both, w3[...], preferred_element_type=F32)
        low = rhs[0:tall] + rhs[tall : 2 * tall]
        high = rhs[2 * tall : 3 * tall] + rhs[3 * tall :]
        lane = lax.broadcasted_iota(jnp.int32, (tall, LANES), 1)
        return jnp.where(lane < 3 * TERMS, low, high)

    def send_sums(late):
        mine_at = sums.at[late * n_chan + me]
        for k in range(1, n_chan):
            pltpu.make_async_remote_copy(
                src_ref=mine_at, dst_ref=mine_at,
                send_sem=sum_send, recv_sem=sum_recv.at[late],
                device_id={"chan": lax.rem(me + k, n_chan)}, device_id_type=MESH,
            ).start()

    count = len(spans)
    lag = min(LAG, count)
    pairs = half // step
    early = jnp.zeros((part, LANES), F32)
    filled = raw.at[:, 0 : (group + 1) * ch]
    for c in range(count + lag):
        if c < count:
            forward_far(c, 0)
        if c == lag:
            pltpu.make_async_copy(filled, filled, own_sem).wait()
        if c < lag:
            for q in range(c * pairs // lag, (c + 1) * pairs // lag):
                weigh(q)
        else:
            process(c - lag)
        if c < count:
            for p in range(1, pieces):
                forward_far(c, p)
        if 2 <= c + 1 < points:
            relay(c + 1)
        if c == lag - 1:
            shape_own()
        if c >= lag:
            done = c - lag
            if done < count - 1 and (count - done) % 2 == 0 and (done > 0 or count < 4):
                first = 0 if done < 3 else done - 1
                found = gather(products(first, done))
                for i in range(first, done + 1):
                    rows_of = found[(i - first) * part : (i - first + 1) * part]
                    early = jnp.where(place == i, rows_of, early)
            if done == count - 2:
                sums[me] = early
                send_sums(0)
    sums[n_chan + me] = products(count - 1, count - 1)
    send_sums(1)

    sided(lambda width: amount(pl.ds(0, rows), (group - 1) * ch + width, near_sem).wait_send())

    def sums_wait(first, blocks, recv):
        ref = sums.at[first : first + blocks]
        return pltpu.make_async_remote_copy(
            src_ref=ref, dst_ref=ref, send_sem=sum_send, recv_sem=recv,
            device_id={"chan": me}, device_id_type=MESH,
        )

    def put_left(start, spread):
        spread = gather(spread)
        hi, mid, lo = (v.astype(F32) for v in split3(spread))
        spot = lax.broadcasted_iota(jnp.int32, spread.shape, 1) // TERMS
        picked = jnp.where(spot == 4, lo, jnp.zeros_like(lo))
        picked = jnp.where((spot == 2) | (spot == 5), mid, picked)
        picked = jnp.where((spot < 2) | (spot == 3), hi, picked)
        left_out[start : start + spread.shape[0], :] = picked.astype(BF16)

    def over_slabs(late, b):
        tot = sums[late * n_chan + b]
        for z in range(1, slabs):
            tot = tot + sums[late * n_chan + z * group + b]
        return tot

    sums_wait(0, n_chan - 1, sum_recv.at[0]).wait_recv()
    for b in range(group):
        tot = over_slabs(0, b)
        put_left(
            b * rows,
            jnp.concatenate([jnp.where(place == c, tot, 0.0) for c in range(count - 1)], axis=0),
        )
    for b in range(group):
        r = slice(b * rows, b * rows + spans[-1][0])
        mine[r, :] = mine[r, :] - jnp.dot(
            left_out[r, :], right_out[...], preferred_element_type=F32
        )
    sums_wait(0, 2 * (n_chan - 1), sum_recv.at[0]).wait_send()
    sums_wait(0, n_chan - 1, sum_recv.at[1]).wait_recv()
    for b in range(group):
        put_left(b * rows + spans[-1][0], over_slabs(1, b))


def subtract(rows, part, cube, left, right, out, buf, sem):
    for start in range(0, cube.shape[0], rows):
        r = pl.ds(start, rows - part)
        pltpu.make_async_copy(cube.at[r, :], out.at[r, :], sem).start()
    for start in range(rows - part, cube.shape[0], rows):
        r = pl.ds(start, part)
        buf[r, :] = cube[r, :] - jnp.dot(left[r, :], right[...], preferred_element_type=F32)
        pltpu.make_async_copy(buf.at[r, :], out.at[r, :], sem).start()
    pltpu.make_async_copy(buf, out, sem).wait()


def per_device(cube, windows, mask):
    pix, ch = cube.shape
    n_chan = lax.axis_size("chan")
    total = ch * n_chan
    group = min(n_chan, max(4, HALO // ch))
    slab_ch = group * ch
    rows = pix // group
    wide = slab_ch + 2 * HALO
    vmem = pl.BlockSpec(memory_space=pltpu.VMEM)
    hbm = pl.BlockSpec(memory_space=pl.ANY)
    dma = pltpu.SemaphoreType.DMA
    chunks = len(chunk_spans(rows))
    part = rows // chunks
    lin = jnp.asarray(linearization())
    depth = 8 * TERMS
    kept = pl.pallas_call(
        functools.partial(kernel, n_chan, group, total),
        out_shape=(
            pltpu.VMEM((pix, depth), BF16),
            pltpu.VMEM((depth, ch), BF16),
            pltpu.VMEM((pix, ch), F32),
        ),
        in_specs=[hbm, hbm, hbm, hbm, hbm],
        out_specs=(vmem, vmem, vmem),
        scratch_shapes=[
            pltpu.SMEM(windows.shape, jnp.int32),
            pltpu.VMEM((total // LANES, LANES), jnp.int32),
            pltpu.VMEM((1, total), jnp.int32),
            pltpu.VMEM(lin.shape, F32),
            pltpu.VMEM((rows, wide), F32),
            pltpu.VMEM((part, wide), F32),
            pltpu.VMEM((part, wide), F32),
            pltpu.VMEM((rows, slab_ch), F32),
            pltpu.VMEM((TERMS, slab_ch), F32),
            pltpu.VMEM((slab_ch // 2, LANES), BF16),
            pltpu.VMEM((2 * n_chan, part, LANES), F32),
            dma((4,)), dma, pltpu.SemaphoreType.REGULAR((2,)), dma, dma,
            dma((chunks, PIECES if ch >= PIECES * LANES else 1)), dma((chunks,)), dma, dma((2,)),
        ],
        compiler_params=pltpu.CompilerParams(
            collective_id=0, has_side_effects=True
        ),
    )(windows, cube, mask.reshape(-1, LANES), mask.reshape(1, total), lin)
    left, right, mine = (pltpu.with_memory_space_constraint(a, pltpu.VMEM) for a in kept)
    return pl.pallas_call(
        functools.partial(subtract, rows, part),
        out_shape=jax.ShapeDtypeStruct((pix, ch), F32),
        in_specs=[vmem, vmem, vmem],
        out_specs=hbm,
        scratch_shapes=[pltpu.VMEM((pix, ch), F32), dma],
    )(mine, left, right)


def solution(mesh):
    placed = (P("pix", "chan"), P(), P())
    return jax.shard_map(
        per_device, mesh=mesh, in_specs=placed, out_specs=P("pix", "chan"), check_vma=False
    )
```

```python
import functools
import math

import jax
import jax.numpy as jnp
import numpy as np
from jax import lax
from jax.experimental import pallas as pl
from jax.experimental.pallas import tpu as pltpu
from jax.sharding import PartitionSpec as P

TERMS = 16
PASSES = 8
WMAX = 1024
HALO = 2 * WMAX
LANES = 128
CHUNKS = 8
LAG = 3
AHEAD = 3
PIECES = 2
LATE = 3
WINDOW = 10
MESH = pl.DeviceIdType.MESH
F32 = jnp.float32
BF16 = jnp.bfloat16


def chunk_spans(rows):
    part = max(8, rows // CHUNKS)
    return [(start, part) for start in range(0, rows, part)]


def linearization():
    def a(r):
        return math.comb(2 * r, r) / 2.0**r

    out = np.zeros((2 * TERMS - 1, TERMS, TERMS))
    for n in range(TERMS):
        for m in range(TERMS):
            for r in range(min(n, m) + 1):
                k = n + m - 2 * r
                out[k, n, m] = (
                    a(r) * a(n - r) * a(m - r) / a(n + m - r)
                    * (2 * k + 1) / (2 * n + 2 * m - 2 * r + 1)
                )
    return out.astype(np.float32)


def next_legendre(order, xvals, here, before):
    return ((2.0 * order + 1.0) * xvals * here - order * before) * (1.0 / (order + 1.0))


def split3(v):
    hi = v.astype(BF16)
    rest = v - hi.astype(F32)
    mid = rest.astype(BF16)
    lo = (rest - mid.astype(F32)).astype(BF16)
    return hi, mid, lo


def kernel(
    n_chan, group, total,
    windows_hbm, cube, mask_sq_hbm, mask_row_hbm, lin_hbm,
    left_out, right_out, mine,
    windows, mask_sq, mask_row, lin, raw, ping, pong, fit, table, w3, sums,
    load_sem, own_sem, token, send_sem, last_sem, near_sem, far_sem, halo_sem, sum_send, sum_recv,
):
    pix, ch = cube.shape
    rows = raw.shape[0]
    slab_ch = group * ch
    tiles = slab_ch // LANES
    slabs = n_chan // group
    spans = chunk_spans(rows)
    last = len(spans) - 2
    order = [*range(last), last + 1, last]
    pieces = far_sem.shape[1]
    bit = ch // pieces
    me = lax.axis_index("chan")
    slab = me // group
    g = lax.rem(me, group)
    own_col = pl.multiple_of(HALO + g * ch, LANES)

    def peer(b):
        return {"chan": slab * group + b}

    own_rows = pl.multiple_of(g * rows, 8)
    barrier = pltpu.get_barrier_semaphore()

    def greet(device):
        pl.semaphore_signal(
            barrier, inc=1, device_id={"chan": device}, device_id_type=MESH
        )

    for k in range(1, group):
        greet(slab * group + lax.rem(g + k, group))

    @pl.when(slab > 0)
    def _():
        greet(me - group)

    @pl.when(slab < slabs - 1)
    def _():
        greet(me + group)

    loads = [
        pltpu.make_async_copy(mask_sq_hbm, mask_sq, load_sem.at[0]),
        pltpu.make_async_copy(mask_row_hbm, mask_row, load_sem.at[1]),
        pltpu.make_async_copy(lin_hbm, lin, load_sem.at[2]),
        pltpu.make_async_copy(windows_hbm, windows, load_sem.at[3]),
    ]
    own = pltpu.make_async_copy(
        cube.at[pl.ds(own_rows, rows), :], raw.at[:, pl.ds(own_col, ch)], own_sem
    )
    kept = pltpu.make_async_copy(cube, mine, own_sem)
    for copy in loads:
        copy.start()
    own.start()

    @pl.when(slab == 0)
    def _():
        raw[:, 0:HALO] = jnp.full((rows, HALO), jnp.inf, F32)

    @pl.when(slab == slabs - 1)
    def _():
        raw[:, HALO + slab_ch :] = jnp.full((rows, HALO), jnp.inf, F32)

    near = group - 1 + jnp.where(slab > 0, 1, 0) + jnp.where(slab < slabs - 1, 1, 0)
    pl.semaphore_wait(barrier, near)

    points = min(slabs, len(spans))

    def relay(point):
        for up in (True, False):
            place = slab if up else slabs - 1 - slab
            sem = token.at[0 if up else 1]
            to = me + group if up else me - group
            turn = (place == point) if point < points - 1 else (place >= point)

            @pl.when(turn)
            def _():
                if point > 0:
                    pl.semaphore_wait(sem, 1)

                @pl.when(place < slabs - 1)
                def _():
                    pl.semaphore_signal(
                        sem, inc=1, device_id={"chan": to}, device_id_type=MESH
                    )

    def chunk(c):
        return pl.ds(*spans[c])

    def remote(src, dst, recv_sem, to, sent=None):
        return pltpu.make_async_remote_copy(
            src_ref=src, dst_ref=dst, recv_sem=recv_sem,
            send_sem=send_sem if sent is None else sent,
            device_id=to, device_id_type=MESH,
        )

    def near_send(b):
        return remote(
            cube.at[b * rows : (b + 1) * rows, :], raw.at[:, pl.ds(own_col, ch)], near_sem, peer(b)
        )

    def far_send(c, p, b):
        return remote(
            cube.at[pl.ds(b * rows + spans[c][0], spans[c][1]), pl.ds(p * bit, bit)],
            raw.at[chunk(c), pl.ds(pl.multiple_of(own_col + p * bit, LANES), bit)],
            far_sem.at[c, p], peer(b),
        )

    def hop(c, b, up, from_own, first=0, width=None):
        width = ch if width is None else width
        col = first + (b * ch - (slab_ch - HALO) if up else HALO + slab_ch + b * ch)
        if from_own:
            src = cube.at[pl.ds(pl.multiple_of(own_rows + spans[c][0], 8), spans[c][1]), :]
        else:
            src = raw.at[chunk(c), pl.ds(HALO + b * ch + first, width)]
        to = {"chan": me + group if up else me - group}
        sent = last_sem if c == last else None
        return remote(src, raw.at[chunk(c), pl.ds(col, width)], halo_sem.at[c], to, sent)

    def amount(r, width, recv_sem, sent=None):
        ref = raw.at[r, 0:width]
        return remote(ref, ref, recv_sem, {"chan": me}, sent)

    def direct(b, up):
        col = b * ch - (slab_ch - HALO) if up else HALO + slab_ch + b * ch
        for to in range(group):
            if to // 2 != b // 2:
                remote(
                    cube.at[pl.ds(to * rows + spans[last][0], spans[last][1]), :],
                    raw.at[chunk(last), pl.ds(col, ch)], halo_sem.at[last],
                    {"chan": (slab + (1 if up else -1)) * group + to}, last_sem,
                ).start()

    def direct_all():
        for b in range(group):
            if goes_up(b):
                @pl.when((g == b) & (slab < slabs - 1))
                def _():
                    direct(b, True)
            if goes_down(b):
                @pl.when((g == b) & (slab > 0))
                def _():
                    direct(b, False)

    def direct_wait():
        for b in range(group):
            beside = [a for a in range(group) if a // 2 == b // 2]
            up = sum(map(goes_up, beside)) + (group - 2) * goes_up(b)
            down = sum(map(goes_down, beside)) + (group - 2) * goes_down(b)
            for blocks, where in (
                (up + down, inner), (up, slab == 0), (down, slab == slabs - 1)
            ):
                if blocks and slabs > 1:
                    @pl.when((g == b) & where)
                    def _():
                        amount(chunk(last), blocks * ch, near_sem, last_sem).wait_send()

    inner = (slab > 0) & (slab < slabs - 1)

    def sided(wait):
        if slabs > 1:
            pl.when(inner)(lambda: wait(2 * HALO))
            pl.when(jnp.logical_not(inner))(lambda: wait(HALO))
        else:
            wait(0)

    def goes_up(b):
        return b * ch >= slab_ch - HALO

    def goes_down(b):
        return b * ch < HALO

    def own_hops(c):
        for b in range(group):
            if goes_up(b):
                @pl.when((g == b) & (slab < slabs - 1))
                def _():
                    hop(c, b, True, True).start()
            if goes_down(b):
                @pl.when((g == b) & (slab > 0))
                def _():
                    hop(c, b, False, True).start()

    def pass_on(c, b, *stretch):
        if goes_up(b):
            @pl.when(slab < slabs - 1)
            def _():
                hop(c, b, True, False, *stretch).start()
        if goes_down(b):
            @pl.when(slab > 0)
            def _():
                hop(c, b, False, False, *stretch).start()

    def forward_near():
        amount(pl.ds(0, rows), ch, near_sem).wait_recv()
        for c in range(len(spans)):
            if c >= AHEAD:
                own_hops(c)
            for b in range(group):
                @pl.when((g != b) & (g // 2 == b // 2))
                def _():
                    pass_on(c, b)

    def feed(c, p):
        for b in range(group):
            @pl.when(g // 2 != b // 2)
            def _():
                far_send(c, p, b).start()

    def forward_far(turn, p):
        c = order[turn]
        amount(chunk(c), (group - 2) * bit, far_sem.at[c, p]).wait_recv()
        for b in range(group):
            if c == last:
                break

            @pl.when(g // 2 != b // 2)
            def _():
                pass_on(c, b, p * bit, bit)
        later = turn * pieces + p + WINDOW
        if later < len(spans) * pieces:
            feed(order[later // pieces], later % pieces)

    def halo_wait(c):
        if slabs > 1:
            sided(lambda width: amount(chunk(c), width, halo_sem.at[c]).wait_recv())

    for c in range(len(spans)):
        for p in range(pieces):
            if c * pieces + p < WINDOW:
                feed(order[c], p)
        if c == 0:
            for b in range(group):
                @pl.when((g != b) & (g // 2 == b // 2))
                def _():
                    near_send(b).start()
        if c < AHEAD:
            own_hops(c)
    relay(0)
    for copy in loads:
        copy.wait()

    shape = mask_sq.shape
    index = lax.broadcasted_iota(jnp.int32, shape, 0) * shape[1] + lax.broadcasted_iota(
        jnp.int32, shape, 1
    )
    xvals = (2.0 * index.astype(F32) + 1.0) * (1.0 / total) - 1.0
    keep = mask_sq[...].astype(F32)
    here, before = jnp.ones_like(xvals), jnp.zeros_like(xvals)
    gram = jnp.zeros((TERMS, TERMS), F32)
    for k in range(2 * TERMS - 1):
        moment = jnp.sum(here * keep, axis=0, keepdims=True)
        moment = jnp.sum(moment, axis=1, keepdims=True)
        gram = gram + moment * lin[k]
        here, before = next_legendre(k, xvals, here, before), here

    row_id = lax.broadcasted_iota(jnp.int32, (TERMS, 2 * TERMS), 0)
    col_id = lax.broadcasted_iota(jnp.int32, (TERMS, 2 * TERMS), 1)
    eye = jnp.where(row_id + TERMS == col_id, 1.0, 0.0).astype(F32)
    aug = eye + jnp.concatenate([gram, jnp.zeros_like(gram)], axis=1)
    for p in range(TERMS):
        lead = aug[p : p + 1, :] / aug[p : p + 1, p : p + 1]
        aug = jnp.where(row_id == p, lead, aug - aug[:, p : p + 1] * lead)
    inverse = aug[:, TERMS:]

    half = slab_ch // 2
    step = min(1024, half)
    base = slab * slab_ch

    def weigh(q):
        parts = []
        for s in (q * step, half + q * step):
            lane = lax.broadcasted_iota(jnp.int32, (1, step), 1)
            x_s = (2.0 * (base + s + lane).astype(F32) + 1.0) * (1.0 / total) - 1.0
            here, before = jnp.ones_like(x_s), jnp.zeros_like(x_s)
            for n in range(TERMS):
                table[n : n + 1, s : s + step] = here
                here, before = next_legendre(n, x_s, here, before), here
            keep_s = mask_row[:, pl.ds(pl.multiple_of(base + s, LANES), step)].astype(F32)
            parts += [v.astype(F32) for v in split3(table[:, s : s + step] * keep_s)]
        parts.append(jnp.zeros((2 * TERMS, step), F32))
        w3[q * step : (q + 1) * step, :] = jnp.concatenate(parts, axis=0).T.astype(BF16)

    def shape_own():
        t_own = table[:, pl.ds(pl.multiple_of(g * ch, LANES), ch)]
        shaped = jnp.zeros_like(t_own)
        for m in range(TERMS):
            shaped = shaped + inverse[:, m : m + 1] * t_own[m : m + 1, :]
        a_hi, a_mid, a_lo = split3(shaped)
        zero = jnp.zeros_like(a_hi)
        right_out[...] = jnp.concatenate(
            [a_hi, a_mid, a_hi, a_lo, a_hi, a_mid, zero, zero], axis=0
        )

    forward_near()
    kept.start()
    if points > 1:
        relay(1)
    edge = HALO // LANES

    def snip(start, block):
        r = pl.ds(start, block)
        lane = lax.broadcasted_iota(jnp.int32, (block, LANES), 1)

        def at(ref, t):
            return ref[0:block, (t + edge) * LANES : (t + edge + 1) * LANES]

        def put(ref, t, v):
            ref[0:block, (t + edge) * LANES : (t + edge + 1) * LANES] = v

        def first(t):
            return raw[r, (t + edge) * LANES : (t + edge + 1) * LANES]

        far = WMAX // LANES
        for t in range(-far, tiles + far):
            put(ping, t, jnp.minimum(first(t), 0.5 * (first(t - far) + first(t + far))))
        src, dst = ping, pong
        for k in range(1, PASSES):
            bound = max(LANES, WMAX >> k)
            b = bound // LANES
            d = bound - windows[k]
            back = lax.rem(LANES - d, LANES)
            low_here = lane < LANES - d
            high_here = lane >= d
            reach = 0 if k == PASSES - 1 else b
            left = {}
            right = {}
            for t in range(-reach, tiles + reach):
                for u in (t - b, t - b + 1):
                    if u not in left:
                        left[u] = pltpu.roll(at(src, u), back, 1)
                for u in (t + b - 1, t + b):
                    if u not in right:
                        right[u] = pltpu.roll(at(src, u), d, 1)
                lower = jnp.where(low_here, left[t - b], left[t - b + 1])
                upper = jnp.where(high_here, right[t + b], right[t + b - 1])
                v = jnp.minimum(at(src, t), 0.5 * (lower + upper))
                if k < PASSES - 1:
                    put(dst, t, v)
                else:
                    cols = slice(t * LANES, (t + 1) * LANES)
                    fit[r, cols] = v
            src, dst = dst, src

    def process(c):
        halo_wait(c)
        snip(*spans[c])

    part = spans[0][1]
    place = lax.broadcasted_iota(jnp.int32, (part, LANES), 1) // TERMS

    def gather(v):
        for shift in (4 * TERMS, 2 * TERMS, TERMS):
            v = v + pltpu.roll(v, shift, 1)
        return v

    def products(first, last):
        tall = (last - first + 1) * part
        whole = fit[spans[first][0] : spans[first][0] + tall, :]
        hi = whole.astype(BF16).astype(F32)
        lo = whole - hi
        both = jnp.concatenate(
            [hi[:, 0:half], lo[:, 0:half], hi[:, half:], lo[:, half:]], axis=0
        ).astype(BF16)
        rhs = jnp.dot(both, w3[...], preferred_element_type=F32)
        low = rhs[0:tall] + rhs[tall : 2 * tall]
        high = rhs[2 * tall : 3 * tall] + rhs[3 * tall :]
        lane = lax.broadcasted_iota(jnp.int32, (tall, LANES), 1)
        return jnp.where(lane < 3 * TERMS, low, high)

    def send_sums(late):
        mine_at = sums.at[pl.ds(n_chan + 2 * me, 2) if late else pl.ds(me, 1)]
        for k in range(1, n_chan):
            pltpu.make_async_remote_copy(
                src_ref=mine_at, dst_ref=mine_at,
                send_sem=sum_send, recv_sem=sum_recv.at[late],
                device_id={"chan": lax.rem(me + k, n_chan)}, device_id_type=MESH,
            ).start()

    count = len(spans)
    lag = min(LAG, count)
    pairs = half // step
    early = jnp.zeros((part, LANES), F32)
    filled = raw.at[:, 0 : (group + 1) * ch]
    for c in range(count + lag):
        if c < count:
            forward_far(c, 0)
        if c == lag:
            pltpu.make_async_copy(filled, filled, own_sem).wait()
        if c < lag:
            for q in range(c * pairs // lag, (c + 1) * pairs // lag):
                weigh(q)
        else:
            process(c - lag)
        if c < count:
            for p in range(1, pieces):
                forward_far(c, p)
        if 2 <= c + 1 < points:
            relay(c + 1)
        if c + 2 == max(points, 3):
            direct_all()
        if c == lag - 1:
            shape_own()
        if c >= lag:
            done = c - lag
            if done < count - 1 and (count - done) % 2 == 0 and (done > 0 or count < 4):
                first = 0 if done < 3 else done - 1
                found = gather(products(first, done))
                for i in range(first, done + 1):
                    rows_of = found[(i - first) * part : (i - first + 1) * part]
                    early = jnp.where(place == i, rows_of, early)
            if done == count - LATE - 1:
                sums[me] = early
                send_sums(0)
            if done == count - 2:
                sums[n_chan + 2 * me] = early
    sums[n_chan + 2 * me + 1] = products(count - 1, count - 1)
    send_sums(1)

    share = rows - spans[last][1]

    def sent_wait(width):
        amount(pl.ds(0, rows), (group - 1) * ch, near_sem).wait_send()
        amount(pl.ds(0, share), width, near_sem).wait_send()

    sided(sent_wait)
    direct_wait()

    def sums_wait(first, blocks, recv):
        ref = sums.at[first : first + blocks]
        return pltpu.make_async_remote_copy(
            src_ref=ref, dst_ref=ref, send_sem=sum_send, recv_sem=recv,
            device_id={"chan": me}, device_id_type=MESH,
        )

    def put_left(start, spread):
        spread = gather(spread)
        hi, mid, lo = (v.astype(F32) for v in split3(spread))
        spot = lax.broadcasted_iota(jnp.int32, spread.shape, 1) // TERMS
        picked = jnp.where(spot == 4, lo, jnp.zeros_like(lo))
        picked = jnp.where((spot == 2) | (spot == 5), mid, picked)
        picked = jnp.where((spot < 2) | (spot == 3), hi, picked)
        left_out[start : start + spread.shape[0], :] = picked.astype(BF16)

    def over_slabs(start, stride, b):
        tot = sums[start + stride * b]
        for z in range(1, slabs):
            tot = tot + sums[start + stride * (z * group + b)]
        return tot

    def apart(tot, first, end):
        return [jnp.where(place == c, tot, 0.0) for c in range(first, end)]

    begun = spans[count - LATE][0]
    sums_wait(0, n_chan - 1, sum_recv.at[0]).wait_recv()
    for b in range(group):
        put_left(
            b * rows,
            jnp.concatenate(apart(over_slabs(0, 1, b), 0, count - LATE), axis=0),
        )
    for b in range(group):
        r = slice(b * rows, b * rows + begun)
        mine[r, :] = mine[r, :] - jnp.dot(
            left_out[r, :], right_out[...], preferred_element_type=F32
        )
    sums_wait(0, 3 * (n_chan - 1), sum_recv.at[0]).wait_send()
    sums_wait(0, 2 * (n_chan - 1), sum_recv.at[1]).wait_recv()
    for b in range(group):
        mid = apart(over_slabs(n_chan, 2, b), count - LATE, count - 1)
        end = over_slabs(n_chan + 1, 2, b)
        put_left(b * rows + begun, jnp.concatenate([*mid, end], axis=0))


def subtract(rows, part, cube, left, right, out, buf, sem):
    for start in range(0, cube.shape[0], rows):
        r = pl.ds(start, rows - part)
        pltpu.make_async_copy(cube.at[r, :], out.at[r, :], sem).start()
    for start in range(rows - part, cube.shape[0], rows):
        r = pl.ds(start, part)
        buf[r, :] = cube[r, :] - jnp.dot(left[r, :], right[...], preferred_element_type=F32)
        pltpu.make_async_copy(buf.at[r, :], out.at[r, :], sem).start()
    pltpu.make_async_copy(buf, out, sem).wait()


def per_device(cube, windows, mask):
    pix, ch = cube.shape
    n_chan = lax.axis_size("chan")
    total = ch * n_chan
    group = min(n_chan, max(4, HALO // ch))
    slab_ch = group * ch
    rows = pix // group
    wide = slab_ch + 2 * HALO
    vmem = pl.BlockSpec(memory_space=pltpu.VMEM)
    hbm = pl.BlockSpec(memory_space=pl.ANY)
    dma = pltpu.SemaphoreType.DMA
    chunks = len(chunk_spans(rows))
    part = rows // chunks
    lin = jnp.asarray(linearization())
    depth = 8 * TERMS
    kept = pl.pallas_call(
        functools.partial(kernel, n_chan, group, total),
        out_shape=(
            pltpu.VMEM((pix, depth), BF16),
            pltpu.VMEM((depth, ch), BF16),
            pltpu.VMEM((pix, ch), F32),
        ),
        in_specs=[hbm, hbm, hbm, hbm, hbm],
        out_specs=(vmem, vmem, vmem),
        scratch_shapes=[
            pltpu.SMEM(windows.shape, jnp.int32),
            pltpu.VMEM((total // LANES, LANES), jnp.int32),
            pltpu.VMEM((1, total), jnp.int32),
            pltpu.VMEM(lin.shape, F32),
            pltpu.VMEM((rows, wide), F32),
            pltpu.VMEM((part, wide), F32),
            pltpu.VMEM((part, wide), F32),
            pltpu.VMEM((rows, slab_ch), F32),
            pltpu.VMEM((TERMS, slab_ch), F32),
            pltpu.VMEM((slab_ch // 2, LANES), BF16),
            pltpu.VMEM((3 * n_chan, part, LANES), F32),
            dma((4,)), dma, pltpu.SemaphoreType.REGULAR((2,)), dma, dma, dma,
            dma((chunks, PIECES if ch >= PIECES * LANES else 1)), dma((chunks,)), dma, dma((2,)),
        ],
        compiler_params=pltpu.CompilerParams(
            collective_id=0, has_side_effects=True
        ),
    )(windows, cube, mask.reshape(-1, LANES), mask.reshape(1, total), lin)
    left, right, mine = (pltpu.with_memory_space_constraint(a, pltpu.VMEM) for a in kept)
    return pl.pallas_call(
        functools.partial(subtract, rows, LATE * part),
        out_shape=jax.ShapeDtypeStruct((pix, ch), F32),
        in_specs=[vmem, vmem, vmem],
        out_specs=hbm,
        scratch_shapes=[pltpu.VMEM((pix, ch), F32), dma],
    )(mine, left, right)


def solution(mesh):
    placed = (P("pix", "chan"), P(), P())
    return jax.shard_map(
        per_device, mesh=mesh, in_specs=placed, out_specs=P("pix", "chan"), check_vma=False
    )
```

```python
import functools
import math

import jax
import jax.numpy as jnp
import numpy as np
from jax import lax
from jax.experimental import pallas as pl
from jax.experimental.pallas import tpu as pltpu
from jax.sharding import PartitionSpec as P

TERMS = 16
PASSES = 8
WMAX = 1024
HALO = 2 * WMAX
LANES = 128
CHUNKS = 8
LAG = 3
AHEAD = 3
PIECES = 2
LATE = 3
WINDOW = 10
MESH = pl.DeviceIdType.MESH
F32 = jnp.float32
BF16 = jnp.bfloat16


def chunk_spans(rows):
    part = max(8, rows // CHUNKS)
    return [(start, part) for start in range(0, rows, part)]


def linearization():
    def a(r):
        return math.comb(2 * r, r) / 2.0**r

    out = np.zeros((2 * TERMS - 1, TERMS, TERMS))
    for n in range(TERMS):
        for m in range(TERMS):
            for r in range(min(n, m) + 1):
                k = n + m - 2 * r
                out[k, n, m] = (
                    a(r) * a(n - r) * a(m - r) / a(n + m - r)
                    * (2 * k + 1) / (2 * n + 2 * m - 2 * r + 1)
                )
    return out.astype(np.float32)


def next_legendre(order, xvals, here, before):
    return ((2.0 * order + 1.0) * xvals * here - order * before) * (1.0 / (order + 1.0))


def split3(v):
    hi = v.astype(BF16)
    rest = v - hi.astype(F32)
    mid = rest.astype(BF16)
    lo = (rest - mid.astype(F32)).astype(BF16)
    return hi, mid, lo


def kernel(
    n_chan, group, total,
    windows_hbm, cube, mask_sq_hbm, mask_row_hbm, lin_hbm,
    left_out, right_out, mine,
    windows, mask_sq, mask_row, lin, raw, ping, pong, fit, table, w3, sums,
    load_sem, own_sem, token, send_sem, last_sem, near_sem, far_sem, halo_sem, sum_send, sum_recv,
):
    pix, ch = cube.shape
    rows = raw.shape[0]
    slab_ch = group * ch
    tiles = slab_ch // LANES
    slabs = n_chan // group
    spans = chunk_spans(rows)
    last = len(spans) - 2
    order = [*range(last), last + 1, last]
    pieces = far_sem.shape[1]
    bit = ch // pieces
    me = lax.axis_index("chan")
    slab = me // group
    g = lax.rem(me, group)
    own_col = pl.multiple_of(HALO + g * ch, LANES)

    def peer(b):
        return {"chan": slab * group + b}

    own_rows = pl.multiple_of(g * rows, 8)
    barrier = pltpu.get_barrier_semaphore()

    def greet(device):
        pl.semaphore_signal(
            barrier, inc=1, device_id={"chan": device}, device_id_type=MESH
        )

    for k in range(1, group):
        greet(slab * group + lax.rem(g + k, group))

    @pl.when(slab > 0)
    def _():
        greet(me - group)

    @pl.when(slab < slabs - 1)
    def _():
        greet(me + group)

    loads = [
        pltpu.make_async_copy(mask_sq_hbm, mask_sq, load_sem.at[0]),
        pltpu.make_async_copy(mask_row_hbm, mask_row, load_sem.at[1]),
        pltpu.make_async_copy(lin_hbm, lin, load_sem.at[2]),
        pltpu.make_async_copy(windows_hbm, windows, load_sem.at[3]),
    ]
    own = pltpu.make_async_copy(
        cube.at[pl.ds(own_rows, rows), :], raw.at[:, pl.ds(own_col, ch)], own_sem
    )
    kept = pltpu.make_async_copy(cube, mine, own_sem)
    for copy in loads:
        copy.start()
    own.start()

    @pl.when(slab == 0)
    def _():
        raw[:, 0:HALO] = jnp.full((rows, HALO), jnp.inf, F32)

    @pl.when(slab == slabs - 1)
    def _():
        raw[:, HALO + slab_ch :] = jnp.full((rows, HALO), jnp.inf, F32)

    near = group - 1 + jnp.where(slab > 0, 1, 0) + jnp.where(slab < slabs - 1, 1, 0)
    pl.semaphore_wait(barrier, near)

    points = min(slabs, len(spans))

    def relay(point):
        for up in (True, False):
            place = slab if up else slabs - 1 - slab
            sem = token.at[0 if up else 1]
            to = me + group if up else me - group
            turn = (place == point) if point < points - 1 else (place >= point)

            @pl.when(turn)
            def _():
                if point > 0:
                    pl.semaphore_wait(sem, 1)

                @pl.when(place < slabs - 1)
                def _():
                    pl.semaphore_signal(
                        sem, inc=1, device_id={"chan": to}, device_id_type=MESH
                    )

    def chunk(c):
        return pl.ds(*spans[c])

    def remote(src, dst, recv_sem, to, sent=None):
        return pltpu.make_async_remote_copy(
            src_ref=src, dst_ref=dst, recv_sem=recv_sem,
            send_sem=send_sem if sent is None else sent,
            device_id=to, device_id_type=MESH,
        )

    def near_send(b):
        return remote(
            cube.at[b * rows : (b + 1) * rows, :], raw.at[:, pl.ds(own_col, ch)], near_sem, peer(b)
        )

    def far_send(c, p, b):
        return remote(
            cube.at[pl.ds(b * rows + spans[c][0], spans[c][1]), pl.ds(p * bit, bit)],
            raw.at[chunk(c), pl.ds(pl.multiple_of(own_col + p * bit, LANES), bit)],
            far_sem.at[c, p], peer(b),
        )

    def hop(c, b, up, from_own, first=0, width=None):
        width = ch if width is None else width
        col = first + (b * ch - (slab_ch - HALO) if up else HALO + slab_ch + b * ch)
        if from_own:
            src = cube.at[pl.ds(pl.multiple_of(own_rows + spans[c][0], 8), spans[c][1]), :]
        else:
            src = raw.at[chunk(c), pl.ds(HALO + b * ch + first, width)]
        to = {"chan": me + group if up else me - group}
        sent = last_sem if c == last else None
        return remote(src, raw.at[chunk(c), pl.ds(col, width)], halo_sem.at[c], to, sent)

    def amount(r, width, recv_sem, sent=None):
        ref = raw.at[r, 0:width]
        return remote(ref, ref, recv_sem, {"chan": me}, sent)

    def direct(b, up):
        col = b * ch - (slab_ch - HALO) if up else HALO + slab_ch + b * ch
        for to in range(group):
            if to // 2 != b // 2:
                remote(
                    cube.at[pl.ds(to * rows + spans[last][0], spans[last][1]), :],
                    raw.at[chunk(last), pl.ds(col, ch)], halo_sem.at[last],
                    {"chan": (slab + (1 if up else -1)) * group + to}, last_sem,
                ).start()

    def direct_all():
        for b in range(group):
            if goes_up(b):
                @pl.when((g == b) & (slab < slabs - 1))
                def _():
                    direct(b, True)
            if goes_down(b):
                @pl.when((g == b) & (slab > 0))
                def _():
                    direct(b, False)

    def direct_wait():
        for b in range(group):
            beside = [a for a in range(group) if a // 2 == b // 2]
            up = sum(map(goes_up, beside)) + (group - 2) * goes_up(b)
            down = sum(map(goes_down, beside)) + (group - 2) * goes_down(b)
            for blocks, where in (
                (up + down, inner), (up, slab == 0), (down, slab == slabs - 1)
            ):
                if blocks and slabs > 1:
                    @pl.when((g == b) & where)
                    def _():
                        amount(chunk(last), blocks * ch, near_sem, last_sem).wait_send()

    inner = (slab > 0) & (slab < slabs - 1)

    def sided(wait):
        if slabs > 1:
            pl.when(inner)(lambda: wait(2 * HALO))
            pl.when(jnp.logical_not(inner))(lambda: wait(HALO))
        else:
            wait(0)

    def goes_up(b):
        return b * ch >= slab_ch - HALO

    def goes_down(b):
        return b * ch < HALO

    def own_hops(c):
        for b in range(group):
            if goes_up(b):
                @pl.when((g == b) & (slab < slabs - 1))
                def _():
                    hop(c, b, True, True).start()
            if goes_down(b):
                @pl.when((g == b) & (slab > 0))
                def _():
                    hop(c, b, False, True).start()

    def pass_on(c, b, *stretch):
        if goes_up(b):
            @pl.when(slab < slabs - 1)
            def _():
                hop(c, b, True, False, *stretch).start()
        if goes_down(b):
            @pl.when(slab > 0)
            def _():
                hop(c, b, False, False, *stretch).start()

    def forward_near():
        amount(pl.ds(0, rows), ch, near_sem).wait_recv()
        for c in range(len(spans)):
            if c >= AHEAD:
                own_hops(c)
            for b in range(group):
                @pl.when((g != b) & (g // 2 == b // 2))
                def _():
                    pass_on(c, b)

    def feed(c, p):
        for b in range(group):
            @pl.when(g // 2 != b // 2)
            def _():
                far_send(c, p, b).start()

    def forward_far(turn, p):
        c = order[turn]
        amount(chunk(c), (group - 2) * bit, far_sem.at[c, p]).wait_recv()
        for b in range(group):
            if c == last:
                break

            @pl.when(g // 2 != b // 2)
            def _():
                pass_on(c, b, p * bit, bit)
        later = turn * pieces + p + WINDOW
        if later < len(spans) * pieces:
            feed(order[later // pieces], later % pieces)

    def halo_wait(c):
        if slabs > 1:
            sided(lambda width: amount(chunk(c), width, halo_sem.at[c]).wait_recv())

    for c in range(len(spans)):
        for p in range(pieces):
            if c * pieces + p < WINDOW:
                feed(order[c], p)
        if c == 0:
            for b in range(group):
                @pl.when((g != b) & (g // 2 == b // 2))
                def _():
                    near_send(b).start()
        if c < AHEAD:
            own_hops(c)
    relay(0)
    for copy in loads:
        copy.wait()

    shape = mask_sq.shape
    index = lax.broadcasted_iota(jnp.int32, shape, 0) * shape[1] + lax.broadcasted_iota(
        jnp.int32, shape, 1
    )
    xvals = (2.0 * index.astype(F32) + 1.0) * (1.0 / total) - 1.0
    keep = mask_sq[...].astype(F32)
    here, before = jnp.ones_like(xvals), jnp.zeros_like(xvals)
    gram = jnp.zeros((TERMS, TERMS), F32)
    for k in range(2 * TERMS - 1):
        moment = jnp.sum(here * keep, axis=0, keepdims=True)
        moment = jnp.sum(moment, axis=1, keepdims=True)
        gram = gram + moment * lin[k]
        here, before = next_legendre(k, xvals, here, before), here

    row_id = lax.broadcasted_iota(jnp.int32, (TERMS, 2 * TERMS), 0)
    col_id = lax.broadcasted_iota(jnp.int32, (TERMS, 2 * TERMS), 1)
    eye = jnp.where(row_id + TERMS == col_id, 1.0, 0.0).astype(F32)
    aug = eye + jnp.concatenate([gram, jnp.zeros_like(gram)], axis=1)
    for p in range(TERMS):
        lead = aug[p : p + 1, :] / aug[p : p + 1, p : p + 1]
        aug = jnp.where(row_id == p, lead, aug - aug[:, p : p + 1] * lead)
    inverse = aug[:, TERMS:]

    half = slab_ch // 2
    step = min(1024, half)
    base = slab * slab_ch

    def weigh(q):
        parts = []
        for s in (q * step, half + q * step):
            lane = lax.broadcasted_iota(jnp.int32, (1, step), 1)
            x_s = (2.0 * (base + s + lane).astype(F32) + 1.0) * (1.0 / total) - 1.0
            here, before = jnp.ones_like(x_s), jnp.zeros_like(x_s)
            for n in range(TERMS):
                table[n : n + 1, s : s + step] = here
                here, before = next_legendre(n, x_s, here, before), here
            keep_s = mask_row[:, pl.ds(pl.multiple_of(base + s, LANES), step)].astype(F32)
            parts += [v.astype(F32) for v in split3(table[:, s : s + step] * keep_s)]
        parts.append(jnp.zeros((2 * TERMS, step), F32))
        w3[q * step : (q + 1) * step, :] = jnp.concatenate(parts, axis=0).T.astype(BF16)

    def shape_own():
        t_own = table[:, pl.ds(pl.multiple_of(g * ch, LANES), ch)]
        shaped = jnp.zeros_like(t_own)
        for m in range(TERMS):
            shaped = shaped + inverse[:, m : m + 1] * t_own[m : m + 1, :]
        a_hi, a_mid, a_lo = split3(shaped)
        zero = jnp.zeros_like(a_hi)
        right_out[...] = jnp.concatenate(
            [a_hi, a_mid, a_hi, a_lo, a_hi, a_mid, zero, zero], axis=0
        )

    forward_near()
    kept.start()
    if points > 1:
        relay(1)
    edge = HALO // LANES

    def snip(start, block):
        r = pl.ds(start, block)
        lane = lax.broadcasted_iota(jnp.int32, (block, LANES), 1)

        def at(ref, t):
            return ref[0:block, (t + edge) * LANES : (t + edge + 1) * LANES]

        def put(ref, t, v):
            ref[0:block, (t + edge) * LANES : (t + edge + 1) * LANES] = v

        def first(t):
            return raw[r, (t + edge) * LANES : (t + edge + 1) * LANES]

        far = WMAX // LANES
        for t in range(-far, tiles + far):
            put(ping, t, jnp.minimum(first(t), 0.5 * (first(t - far) + first(t + far))))
        src, dst = ping, pong
        for k in range(1, PASSES):
            bound = max(LANES, WMAX >> k)
            b = bound // LANES
            d = bound - windows[k]
            back = lax.rem(LANES - d, LANES)
            low_here = lane < LANES - d
            high_here = lane >= d
            reach = 0 if k == PASSES - 1 else b
            left = {}
            right = {}
            for t in range(-reach, tiles + reach):
                for u in (t - b, t - b + 1):
                    if u not in left:
                        left[u] = pltpu.roll(at(src, u), back, 1)
                for u in (t + b - 1, t + b):
                    if u not in right:
                        right[u] = pltpu.roll(at(src, u), d, 1)
                lower = jnp.where(low_here, left[t - b], left[t - b + 1])
                upper = jnp.where(high_here, right[t + b], right[t + b - 1])
                v = jnp.minimum(at(src, t), 0.5 * (lower + upper))
                if k < PASSES - 1:
                    put(dst, t, v)
                else:
                    cols = slice(t * LANES, (t + 1) * LANES)
                    fit[r, cols] = v
            src, dst = dst, src

    def process(c):
        halo_wait(c)
        snip(*spans[c])

    part = spans[0][1]
    place = lax.broadcasted_iota(jnp.int32, (part, LANES), 1) // TERMS

    def gather(v):
        for shift in (4 * TERMS, 2 * TERMS, TERMS):
            v = v + pltpu.roll(v, shift, 1)
        return v

    def products(first, last):
        tall = (last - first + 1) * part
        whole = fit[spans[first][0] : spans[first][0] + tall, :]
        hi = whole.astype(BF16).astype(F32)
        lo = whole - hi
        both = jnp.concatenate(
            [hi[:, 0:half], lo[:, 0:half], hi[:, half:], lo[:, half:]], axis=0
        ).astype(BF16)
        rhs = jnp.dot(both, w3[...], preferred_element_type=F32)
        low = rhs[0:tall] + rhs[tall : 2 * tall]
        high = rhs[2 * tall : 3 * tall] + rhs[3 * tall :]
        lane = lax.broadcasted_iota(jnp.int32, (tall, LANES), 1)
        return jnp.where(lane < 3 * TERMS, low, high)

    def send_sums(late):
        mine_at = sums.at[late * n_chan + me]
        for k in range(1, n_chan):
            pltpu.make_async_remote_copy(
                src_ref=mine_at, dst_ref=mine_at,
                send_sem=sum_send, recv_sem=sum_recv.at[late],
                device_id={"chan": lax.rem(me + k, n_chan)}, device_id_type=MESH,
            ).start()

    count = len(spans)
    lag = min(LAG, count)
    pairs = half // step
    early = jnp.zeros((part, LANES), F32)

    def spot_of(c):
        return c if c < count - LATE else c - (count - LATE) + 6

    filled = raw.at[:, 0 : (group + 1) * ch]
    for c in range(count + lag):
        if c < count:
            forward_far(c, 0)
        if c == lag:
            pltpu.make_async_copy(filled, filled, own_sem).wait()
        if c < lag:
            for q in range(c * pairs // lag, (c + 1) * pairs // lag):
                weigh(q)
        else:
            process(c - lag)
        if c < count:
            for p in range(1, pieces):
                forward_far(c, p)
        if 2 <= c + 1 < points:
            relay(c + 1)
        if c + 2 == max(points, 3):
            direct_all()
        if c == lag - 1:
            shape_own()
        if c >= lag:
            done = c - lag
            if done < count - 1 and (count - done) % 2 == 0 and (done > 0 or count < 4):
                first = 0 if done < 3 else done - 1
                found = gather(products(first, done))
                for i in range(first, done + 1):
                    rows_of = found[(i - first) * part : (i - first + 1) * part]
                    early = jnp.where(place == spot_of(i), rows_of, early)
            if done == count - LATE - 1:
                sums[me] = early
                send_sums(0)
    found = products(count - 1, count - 1)
    sums[n_chan + me] = jnp.where(place < 6, found, early)
    send_sums(1)

    share = rows - spans[last][1]

    def sent_wait(width):
        amount(pl.ds(0, rows), (group - 1) * ch, near_sem).wait_send()
        amount(pl.ds(0, share), width, near_sem).wait_send()

    sided(sent_wait)
    direct_wait()

    def sums_wait(first, blocks, recv):
        ref = sums.at[first : first + blocks]
        return pltpu.make_async_remote_copy(
            src_ref=ref, dst_ref=ref, send_sem=sum_send, recv_sem=recv,
            device_id={"chan": me}, device_id_type=MESH,
        )

    def put_left(start, spread):
        spread = gather(spread)
        hi, mid, lo = (v.astype(F32) for v in split3(spread))
        spot = lax.broadcasted_iota(jnp.int32, spread.shape, 1) // TERMS
        picked = jnp.where(spot == 4, lo, jnp.zeros_like(lo))
        picked = jnp.where((spot == 2) | (spot == 5), mid, picked)
        picked = jnp.where((spot < 2) | (spot == 3), hi, picked)
        left_out[start : start + spread.shape[0], :] = picked.astype(BF16)

    def over_slabs(late, b):
        tot = sums[late * n_chan + b]
        for z in range(1, slabs):
            tot = tot + sums[late * n_chan + z * group + b]
        return tot

    def apart(tot, first, end):
        return [jnp.where(place == spot_of(c), tot, 0.0) for c in range(first, end)]

    begun = spans[count - LATE][0]
    sums_wait(0, n_chan - 1, sum_recv.at[0]).wait_recv()
    for b in range(group):
        put_left(
            b * rows,
            jnp.concatenate(apart(over_slabs(0, b), 0, count - LATE), axis=0),
        )
    for b in range(group):
        r = slice(b * rows, b * rows + begun)
        mine[r, :] = mine[r, :] - jnp.dot(
            left_out[r, :], right_out[...], preferred_element_type=F32
        )
    sums_wait(0, 2 * (n_chan - 1), sum_recv.at[0]).wait_send()
    sums_wait(0, n_chan - 1, sum_recv.at[1]).wait_recv()
    for b in range(group):
        tot = over_slabs(1, b)
        mid = apart(tot, count - LATE, count - 1)
        end = jnp.where(place < 6, tot, 0.0)
        put_left(b * rows + begun, jnp.concatenate([*mid, end], axis=0))


def subtract(rows, part, cube, left, right, out, buf, sem):
    for start in range(0, cube.shape[0], rows):
        r = pl.ds(start, rows - part)
        pltpu.make_async_copy(cube.at[r, :], out.at[r, :], sem).start()
    for start in range(rows - part, cube.shape[0], rows):
        r = pl.ds(start, part)
        buf[r, :] = cube[r, :] - jnp.dot(left[r, :], right[...], preferred_element_type=F32)
        pltpu.make_async_copy(buf.at[r, :], out.at[r, :], sem).start()
    pltpu.make_async_copy(buf, out, sem).wait()


def per_device(cube, windows, mask):
    pix, ch = cube.shape
    n_chan = lax.axis_size("chan")
    total = ch * n_chan
    group = min(n_chan, max(4, HALO // ch))
    slab_ch = group * ch
    rows = pix // group
    wide = slab_ch + 2 * HALO
    vmem = pl.BlockSpec(memory_space=pltpu.VMEM)
    hbm = pl.BlockSpec(memory_space=pl.ANY)
    dma = pltpu.SemaphoreType.DMA
    chunks = len(chunk_spans(rows))
    part = rows // chunks
    lin = jnp.asarray(linearization())
    depth = 8 * TERMS
    kept = pl.pallas_call(
        functools.partial(kernel, n_chan, group, total),
        out_shape=(
            pltpu.VMEM((pix, depth), BF16),
            pltpu.VMEM((depth, ch), BF16),
            pltpu.VMEM((pix, ch), F32),
        ),
        in_specs=[hbm, hbm, hbm, hbm, hbm],
        out_specs=(vmem, vmem, vmem),
        scratch_shapes=[
            pltpu.SMEM(windows.shape, jnp.int32),
            pltpu.VMEM((total // LANES, LANES), jnp.int32),
            pltpu.VMEM((1, total), jnp.int32),
            pltpu.VMEM(lin.shape, F32),
            pltpu.VMEM((rows, wide), F32),
            pltpu.VMEM((part, wide), F32),
            pltpu.VMEM((part, wide), F32),
            pltpu.VMEM((rows, slab_ch), F32),
            pltpu.VMEM((TERMS, slab_ch), F32),
            pltpu.VMEM((slab_ch // 2, LANES), BF16),
            pltpu.VMEM((2 * n_chan, part, LANES), F32),
            dma((4,)), dma, pltpu.SemaphoreType.REGULAR((2,)), dma, dma, dma,
            dma((chunks, PIECES if ch >= PIECES * LANES else 1)), dma((chunks,)), dma, dma((2,)),
        ],
        compiler_params=pltpu.CompilerParams(
            collective_id=0, has_side_effects=True
        ),
    )(windows, cube, mask.reshape(-1, LANES), mask.reshape(1, total), lin)
    left, right, mine = (pltpu.with_memory_space_constraint(a, pltpu.VMEM) for a in kept)
    return pl.pallas_call(
        functools.partial(subtract, rows, LATE * part),
        out_shape=jax.ShapeDtypeStruct((pix, ch), F32),
        in_specs=[vmem, vmem, vmem],
        out_specs=hbm,
        scratch_shapes=[pltpu.VMEM((pix, ch), F32), dma],
    )(mine, left, right)


def solution(mesh):
    placed = (P("pix", "chan"), P(), P())
    return jax.shard_map(
        per_device, mesh=mesh, in_specs=placed, out_specs=P("pix", "chan"), check_vma=False
    )
```

```python
import functools
import math

import jax
import jax.numpy as jnp
import numpy as np
from jax import lax
from jax.experimental import pallas as pl
from jax.experimental.pallas import tpu as pltpu
from jax.sharding import PartitionSpec as P

TERMS = 16
PASSES = 8
WMAX = 1024
HALO = 2 * WMAX
LANES = 128
CHUNKS = 8
LAG = 3
AHEAD = 3
PIECES = 2
LATE = 3
WINDOW = 10
MESH = pl.DeviceIdType.MESH
F32 = jnp.float32
BF16 = jnp.bfloat16


def chunk_spans(rows):
    part = max(8, rows // CHUNKS)
    return [(start, part) for start in range(0, rows, part)]


def linearization():
    def a(r):
        return math.comb(2 * r, r) / 2.0**r

    out = np.zeros((2 * TERMS - 1, TERMS, TERMS))
    for n in range(TERMS):
        for m in range(TERMS):
            for r in range(min(n, m) + 1):
                k = n + m - 2 * r
                out[k, n, m] = (
                    a(r) * a(n - r) * a(m - r) / a(n + m - r)
                    * (2 * k + 1) / (2 * n + 2 * m - 2 * r + 1)
                )
    return out.astype(np.float32)


def next_legendre(order, xvals, here, before):
    return ((2.0 * order + 1.0) * xvals * here - order * before) * (1.0 / (order + 1.0))


def split3(v):
    hi = v.astype(BF16)
    rest = v - hi.astype(F32)
    mid = rest.astype(BF16)
    lo = (rest - mid.astype(F32)).astype(BF16)
    return hi, mid, lo


def kernel(
    n_chan, group, total,
    windows_hbm, cube, mask_sq_hbm, mask_row_hbm, lin_hbm,
    left_out, right_out, mine,
    windows, mask_sq, mask_row, lin, raw, ping, pong, fit, table, w3, sums,
    load_sem, own_sem, token, send_sem, last_sem, near_sem, far_sem, halo_sem, sum_send, sum_recv,
):
    pix, ch = cube.shape
    rows = raw.shape[0]
    slab_ch = group * ch
    tiles = slab_ch // LANES
    slabs = n_chan // group
    spans = chunk_spans(rows)
    last = len(spans) - 2
    order = [*range(last), last + 1, last]
    pieces = far_sem.shape[1]
    bit = ch // pieces
    me = lax.axis_index("chan")
    slab = me // group
    g = lax.rem(me, group)
    own_col = pl.multiple_of(HALO + g * ch, LANES)

    def peer(b):
        return {"chan": slab * group + b}

    own_rows = pl.multiple_of(g * rows, 8)
    barrier = pltpu.get_barrier_semaphore()

    def greet(device):
        pl.semaphore_signal(
            barrier, inc=1, device_id={"chan": device}, device_id_type=MESH
        )

    for k in range(1, group):
        greet(slab * group + lax.rem(g + k, group))

    @pl.when(slab > 0)
    def _():
        greet(me - group)

    @pl.when(slab < slabs - 1)
    def _():
        greet(me + group)

    loads = [
        pltpu.make_async_copy(mask_sq_hbm, mask_sq, load_sem.at[0]),
        pltpu.make_async_copy(mask_row_hbm, mask_row, load_sem.at[1]),
        pltpu.make_async_copy(lin_hbm, lin, load_sem.at[2]),
        pltpu.make_async_copy(windows_hbm, windows, load_sem.at[3]),
    ]
    own = pltpu.make_async_copy(
        cube.at[pl.ds(own_rows, rows), :], raw.at[:, pl.ds(own_col, ch)], own_sem
    )
    kept = pltpu.make_async_copy(cube, mine, own_sem)
    for copy in loads:
        copy.start()
    own.start()

    @pl.when(slab == 0)
    def _():
        raw[:, 0:HALO] = jnp.full((rows, HALO), jnp.inf, F32)

    @pl.when(slab == slabs - 1)
    def _():
        raw[:, HALO + slab_ch :] = jnp.full((rows, HALO), jnp.inf, F32)

    near = group - 1 + jnp.where(slab > 0, 1, 0) + jnp.where(slab < slabs - 1, 1, 0)
    pl.semaphore_wait(barrier, near)

    points = min(slabs, len(spans))

    def relay(point):
        for up in (True, False):
            place = slab if up else slabs - 1 - slab
            sem = token.at[0 if up else 1]
            to = me + group if up else me - group
            turn = (place == point) if point < points - 1 else (place >= point)

            @pl.when(turn)
            def _():
                if point > 0:
                    pl.semaphore_wait(sem, 1)

                @pl.when(place < slabs - 1)
                def _():
                    pl.semaphore_signal(
                        sem, inc=1, device_id={"chan": to}, device_id_type=MESH
                    )

    def chunk(c):
        return pl.ds(*spans[c])

    def remote(src, dst, recv_sem, to, sent=None):
        return pltpu.make_async_remote_copy(
            src_ref=src, dst_ref=dst, recv_sem=recv_sem,
            send_sem=send_sem if sent is None else sent,
            device_id=to, device_id_type=MESH,
        )

    def near_send(b):
        return remote(
            cube.at[b * rows : (b + 1) * rows, :], raw.at[:, pl.ds(own_col, ch)], near_sem, peer(b)
        )

    def far_send(c, p, b):
        return remote(
            cube.at[pl.ds(b * rows + spans[c][0], spans[c][1]), pl.ds(p * bit, bit)],
            raw.at[chunk(c), pl.ds(pl.multiple_of(own_col + p * bit, LANES), bit)],
            far_sem.at[c, p], peer(b),
        )

    def hop(c, b, up, from_own, first=0, width=None):
        width = ch if width is None else width
        col = first + (b * ch - (slab_ch - HALO) if up else HALO + slab_ch + b * ch)
        if from_own:
            src = cube.at[pl.ds(pl.multiple_of(own_rows + spans[c][0], 8), spans[c][1]), :]
        else:
            src = raw.at[chunk(c), pl.ds(HALO + b * ch + first, width)]
        to = {"chan": me + group if up else me - group}
        sent = last_sem if c == last else None
        return remote(src, raw.at[chunk(c), pl.ds(col, width)], halo_sem.at[c], to, sent)

    def amount(r, width, recv_sem, sent=None):
        ref = raw.at[r, 0:width]
        return remote(ref, ref, recv_sem, {"chan": me}, sent)

    def direct(b, up):
        col = b * ch - (slab_ch - HALO) if up else HALO + slab_ch + b * ch
        for to in range(group):
            if to // 2 != b // 2:
                remote(
                    cube.at[pl.ds(to * rows + spans[last][0], spans[last][1]), :],
                    raw.at[chunk(last), pl.ds(col, ch)], halo_sem.at[last],
                    {"chan": (slab + (1 if up else -1)) * group + to}, last_sem,
                ).start()

    def direct_all():
        for b in range(group):
            if goes_up(b):
                @pl.when((g == b) & (slab < slabs - 1))
                def _():
                    direct(b, True)
            if goes_down(b):
                @pl.when((g == b) & (slab > 0))
                def _():
                    direct(b, False)

    def direct_wait():
        for b in range(group):
            beside = [a for a in range(group) if a // 2 == b // 2]
            up = sum(map(goes_up, beside)) + (group - 2) * goes_up(b)
            down = sum(map(goes_down, beside)) + (group - 2) * goes_down(b)
            for blocks, where in (
                (up + down, inner), (up, slab == 0), (down, slab == slabs - 1)
            ):
                if blocks and slabs > 1:
                    @pl.when((g == b) & where)
                    def _():
                        amount(chunk(last), blocks * ch, near_sem, last_sem).wait_send()

    inner = (slab > 0) & (slab < slabs - 1)

    def sided(wait):
        if slabs > 1:
            pl.when(inner)(lambda: wait(2 * HALO))
            pl.when(jnp.logical_not(inner))(lambda: wait(HALO))
        else:
            wait(0)

    def goes_up(b):
        return b * ch >= slab_ch - HALO

    def goes_down(b):
        return b * ch < HALO

    def own_hops(c):
        for b in range(group):
            if goes_up(b):
                @pl.when((g == b) & (slab < slabs - 1))
                def _():
                    hop(c, b, True, True).start()
            if goes_down(b):
                @pl.when((g == b) & (slab > 0))
                def _():
                    hop(c, b, False, True).start()

    def pass_on(c, b, *stretch):
        if goes_up(b):
            @pl.when(slab < slabs - 1)
            def _():
                hop(c, b, True, False, *stretch).start()
        if goes_down(b):
            @pl.when(slab > 0)
            def _():
                hop(c, b, False, False, *stretch).start()

    def forward_near():
        amount(pl.ds(0, rows), ch, near_sem).wait_recv()
        for c in range(len(spans)):
            if c >= AHEAD:
                own_hops(c)
            for b in range(group):
                @pl.when((g != b) & (g // 2 == b // 2))
                def _():
                    pass_on(c, b)

    def feed(c, p):
        for b in range(group):
            @pl.when(g // 2 != b // 2)
            def _():
                far_send(c, p, b).start()

    def forward_far(turn, p):
        c = order[turn]
        amount(chunk(c), (group - 2) * bit, far_sem.at[c, p]).wait_recv()
        for b in range(group):
            if c == last:
                break

            @pl.when(g // 2 != b // 2)
            def _():
                pass_on(c, b, p * bit, bit)
        later = turn * pieces + p + WINDOW
        if later < len(spans) * pieces:
            feed(order[later // pieces], later % pieces)

    def halo_wait(c):
        if slabs > 1:
            sided(lambda width: amount(chunk(c), width, halo_sem.at[c]).wait_recv())

    for c in range(len(spans)):
        for p in range(pieces):
            if c * pieces + p < WINDOW:
                feed(order[c], p)
        if c == 0:
            for b in range(group):
                @pl.when((g != b) & (g // 2 == b // 2))
                def _():
                    near_send(b).start()
        if c < AHEAD:
            own_hops(c)
    relay(0)
    for copy in loads:
        copy.wait()

    shape = mask_sq.shape
    index = lax.broadcasted_iota(jnp.int32, shape, 0) * shape[1] + lax.broadcasted_iota(
        jnp.int32, shape, 1
    )
    xvals = (2.0 * index.astype(F32) + 1.0) * (1.0 / total) - 1.0
    keep = mask_sq[...].astype(F32)
    here, before = jnp.ones_like(xvals), jnp.zeros_like(xvals)
    gram = jnp.zeros((TERMS, TERMS), F32)
    for k in range(2 * TERMS - 1):
        moment = jnp.sum(here * keep, axis=0, keepdims=True)
        moment = jnp.sum(moment, axis=1, keepdims=True)
        gram = gram + moment * lin[k]
        here, before = next_legendre(k, xvals, here, before), here

    row_id = lax.broadcasted_iota(jnp.int32, (TERMS, 2 * TERMS), 0)
    col_id = lax.broadcasted_iota(jnp.int32, (TERMS, 2 * TERMS), 1)
    eye = jnp.where(row_id + TERMS == col_id, 1.0, 0.0).astype(F32)
    aug = eye + jnp.concatenate([gram, jnp.zeros_like(gram)], axis=1)
    for p in range(TERMS):
        lead = aug[p : p + 1, :] / aug[p : p + 1, p : p + 1]
        aug = jnp.where(row_id == p, lead, aug - aug[:, p : p + 1] * lead)
    inverse = aug[:, TERMS:]

    half = slab_ch // 2
    step = min(1024, half)
    base = slab * slab_ch

    def weigh(q):
        parts = []
        for s in (q * step, half + q * step):
            lane = lax.broadcasted_iota(jnp.int32, (1, step), 1)
            x_s = (2.0 * (base + s + lane).astype(F32) + 1.0) * (1.0 / total) - 1.0
            here, before = jnp.ones_like(x_s), jnp.zeros_like(x_s)
            for n in range(TERMS):
                table[n : n + 1, s : s + step] = here
                here, before = next_legendre(n, x_s, here, before), here
            keep_s = mask_row[:, pl.ds(pl.multiple_of(base + s, LANES), step)].astype(F32)
            parts += [v.astype(F32) for v in split3(table[:, s : s + step] * keep_s)]
        parts.append(jnp.zeros((2 * TERMS, step), F32))
        w3[q * step : (q + 1) * step, :] = jnp.concatenate(parts, axis=0).T.astype(BF16)

    def shape_own():
        t_own = table[:, pl.ds(pl.multiple_of(g * ch, LANES), ch)]
        shaped = jnp.zeros_like(t_own)
        for m in range(TERMS):
            shaped = shaped + inverse[:, m : m + 1] * t_own[m : m + 1, :]
        a_hi, a_mid, a_lo = split3(shaped)
        zero = jnp.zeros_like(a_hi)
        right_out[...] = jnp.concatenate(
            [a_hi, a_mid, a_hi, a_lo, a_hi, a_mid, zero, zero], axis=0
        )

    forward_near()
    kept.start()
    if points > 1:
        relay(1)
    edge = HALO // LANES

    def snip(start, block):
        r = pl.ds(start, block)
        lane = lax.broadcasted_iota(jnp.int32, (block, LANES), 1)

        def at(ref, t):
            return ref[0:block, (t + edge) * LANES : (t + edge + 1) * LANES]

        def put(ref, t, v):
            ref[0:block, (t + edge) * LANES : (t + edge + 1) * LANES] = v

        def first(t):
            return raw[r, (t + edge) * LANES : (t + edge + 1) * LANES]

        far = WMAX // LANES
        for t in range(-far, tiles + far):
            put(ping, t, jnp.minimum(first(t), 0.5 * (first(t - far) + first(t + far))))
        src, dst = ping, pong
        for k in range(1, PASSES):
            bound = max(LANES, WMAX >> k)
            b = bound // LANES
            d = bound - windows[k]
            back = lax.rem(LANES - d, LANES)
            low_here = lane < LANES - d
            high_here = lane >= d
            reach = 0 if k == PASSES - 1 else b
            left = {}
            right = {}
            for t in range(-reach, tiles + reach):
                for u in (t - b, t - b + 1):
                    if u not in left:
                        left[u] = pltpu.roll(at(src, u), back, 1)
                for u in (t + b - 1, t + b):
                    if u not in right:
                        right[u] = pltpu.roll(at(src, u), d, 1)
                lower = jnp.where(low_here, left[t - b], left[t - b + 1])
                upper = jnp.where(high_here, right[t + b], right[t + b - 1])
                v = jnp.minimum(at(src, t), 0.5 * (lower + upper))
                if k < PASSES - 1:
                    put(dst, t, v)
                else:
                    cols = slice(t * LANES, (t + 1) * LANES)
                    fit[r, cols] = v
            src, dst = dst, src

    def process(c):
        halo_wait(c)
        snip(*spans[c])

    part = spans[0][1]
    place = lax.broadcasted_iota(jnp.int32, (part, LANES), 1) // TERMS

    def gather(v):
        for shift in (4 * TERMS, 2 * TERMS, TERMS):
            v = v + pltpu.roll(v, shift, 1)
        return v

    def products(first, last):
        tall = (last - first + 1) * part
        whole = fit[spans[first][0] : spans[first][0] + tall, :]
        hi = whole.astype(BF16).astype(F32)
        lo = whole - hi
        both = jnp.concatenate(
            [hi[:, 0:half], lo[:, 0:half], hi[:, half:], lo[:, half:]], axis=0
        ).astype(BF16)
        rhs = jnp.dot(both, w3[...], preferred_element_type=F32)
        low = rhs[0:tall] + rhs[tall : 2 * tall]
        high = rhs[2 * tall : 3 * tall] + rhs[3 * tall :]
        lane = lax.broadcasted_iota(jnp.int32, (tall, LANES), 1)
        return jnp.where(lane < 3 * TERMS, low, high)

    def send_sums(late):
        mine_at = sums.at[late * n_chan + me]
        for k in range(1, n_chan):
            pltpu.make_async_remote_copy(
                src_ref=mine_at, dst_ref=mine_at,
                send_sem=sum_send, recv_sem=sum_recv.at[late],
                device_id={"chan": lax.rem(me + k, n_chan)}, device_id_type=MESH,
            ).start()

    count = len(spans)
    lag = min(LAG, count)
    pairs = half // step
    early = jnp.zeros((part, LANES), F32)

    def spot_of(c):
        return c if c < count - LATE else c - (count - LATE) + 6

    filled = raw.at[:, 0 : (group + 1) * ch]
    for c in range(count + lag):
        if c < count:
            forward_far(c, 0)
        if c == lag:
            pltpu.make_async_copy(filled, filled, own_sem).wait()
        if c < lag:
            for q in range(c * pairs // lag, (c + 1) * pairs // lag):
                weigh(q)
        else:
            process(c - lag)
        if c < count:
            for p in range(1, pieces):
                forward_far(c, p)
        if 2 <= c + 1 < points:
            relay(c + 1)
        if c + 2 == max(points, 3):
            direct_all()
        if c == lag - 1:
            shape_own()
        if c >= lag:
            done = c - lag
            if done < count - LATE and (count - done) % 2 == 0 and (done > 0 or count < 4):
                first = 0 if done < 3 else done - 1
                found = gather(products(first, done))
                for i in range(first, done + 1):
                    rows_of = found[(i - first) * part : (i - first + 1) * part]
                    early = jnp.where(place == spot_of(i), rows_of, early)
            if done == count - LATE - 1:
                sums[me] = early
                send_sums(0)
    found = products(count - LATE, count - 1)
    done = gather(found[: (LATE - 1) * part])
    tile = jnp.where(place < 6, found[(LATE - 1) * part :], 0.0)
    for i in range(LATE - 1):
        tile = jnp.where(place == 6 + i, done[i * part : (i + 1) * part], tile)
    sums[n_chan + me] = tile
    send_sums(1)

    share = rows - spans[last][1]

    def sent_wait(width):
        amount(pl.ds(0, rows), (group - 1) * ch, near_sem).wait_send()
        amount(pl.ds(0, share), width, near_sem).wait_send()

    sided(sent_wait)
    direct_wait()

    def sums_wait(first, blocks, recv):
        ref = sums.at[first : first + blocks]
        return pltpu.make_async_remote_copy(
            src_ref=ref, dst_ref=ref, send_sem=sum_send, recv_sem=recv,
            device_id={"chan": me}, device_id_type=MESH,
        )

    def put_left(start, spread):
        spread = gather(spread)
        hi, mid, lo = (v.astype(F32) for v in split3(spread))
        spot = lax.broadcasted_iota(jnp.int32, spread.shape, 1) // TERMS
        picked = jnp.where(spot == 4, lo, jnp.zeros_like(lo))
        picked = jnp.where((spot == 2) | (spot == 5), mid, picked)
        picked = jnp.where((spot < 2) | (spot == 3), hi, picked)
        left_out[start : start + spread.shape[0], :] = picked.astype(BF16)

    def over_slabs(late, b):
        tot = sums[late * n_chan + b]
        for z in range(1, slabs):
            tot = tot + sums[late * n_chan + z * group + b]
        return tot

    def apart(tot, first, end):
        return [jnp.where(place == spot_of(c), tot, 0.0) for c in range(first, end)]

    begun = spans[count - LATE][0]
    sums_wait(0, n_chan - 1, sum_recv.at[0]).wait_recv()
    for b in range(group):
        put_left(
            b * rows,
            jnp.concatenate(apart(over_slabs(0, b), 0, count - LATE), axis=0),
        )
    for b in range(group):
        r = slice(b * rows, b * rows + begun)
        mine[r, :] = mine[r, :] - jnp.dot(
            left_out[r, :], right_out[...], preferred_element_type=F32
        )
    sums_wait(0, 2 * (n_chan - 1), sum_recv.at[0]).wait_send()
    sums_wait(0, n_chan - 1, sum_recv.at[1]).wait_recv()
    for b in range(group):
        tot = over_slabs(1, b)
        mid = apart(tot, count - LATE, count - 1)
        end = jnp.where(place < 6, tot, 0.0)
        put_left(b * rows + begun, jnp.concatenate([*mid, end], axis=0))


def subtract(rows, part, cube, left, right, out, buf, sem):
    for start in range(0, cube.shape[0], rows):
        r = pl.ds(start, rows - part)
        pltpu.make_async_copy(cube.at[r, :], out.at[r, :], sem).start()
    for start in range(rows - part, cube.shape[0], rows):
        r = pl.ds(start, part)
        buf[r, :] = cube[r, :] - jnp.dot(left[r, :], right[...], preferred_element_type=F32)
        pltpu.make_async_copy(buf.at[r, :], out.at[r, :], sem).start()
    pltpu.make_async_copy(buf, out, sem).wait()


def per_device(cube, windows, mask):
    pix, ch = cube.shape
    n_chan = lax.axis_size("chan")
    total = ch * n_chan
    group = min(n_chan, max(4, HALO // ch))
    slab_ch = group * ch
    rows = pix // group
    wide = slab_ch + 2 * HALO
    vmem = pl.BlockSpec(memory_space=pltpu.VMEM)
    hbm = pl.BlockSpec(memory_space=pl.ANY)
    dma = pltpu.SemaphoreType.DMA
    chunks = len(chunk_spans(rows))
    part = rows // chunks
    lin = jnp.asarray(linearization())
    depth = 8 * TERMS
    kept = pl.pallas_call(
        functools.partial(kernel, n_chan, group, total),
        out_shape=(
            pltpu.VMEM((pix, depth), BF16),
            pltpu.VMEM((depth, ch), BF16),
            pltpu.VMEM((pix, ch), F32),
        ),
        in_specs=[hbm, hbm, hbm, hbm, hbm],
        out_specs=(vmem, vmem, vmem),
        scratch_shapes=[
            pltpu.SMEM(windows.shape, jnp.int32),
            pltpu.VMEM((total // LANES, LANES), jnp.int32),
            pltpu.VMEM((1, total), jnp.int32),
            pltpu.VMEM(lin.shape, F32),
            pltpu.VMEM((rows, wide), F32),
            pltpu.VMEM((part, wide), F32),
            pltpu.VMEM((part, wide), F32),
            pltpu.VMEM((rows, slab_ch), F32),
            pltpu.VMEM((TERMS, slab_ch), F32),
            pltpu.VMEM((slab_ch // 2, LANES), BF16),
            pltpu.VMEM((2 * n_chan, part, LANES), F32),
            dma((4,)), dma, pltpu.SemaphoreType.REGULAR((2,)), dma, dma, dma,
            dma((chunks, PIECES if ch >= PIECES * LANES else 1)), dma((chunks,)), dma, dma((2,)),
        ],
        compiler_params=pltpu.CompilerParams(
            collective_id=0, has_side_effects=True
        ),
    )(windows, cube, mask.reshape(-1, LANES), mask.reshape(1, total), lin)
    left, right, mine = (pltpu.with_memory_space_constraint(a, pltpu.VMEM) for a in kept)
    return pl.pallas_call(
        functools.partial(subtract, rows, LATE * part),
        out_shape=jax.ShapeDtypeStruct((pix, ch), F32),
        in_specs=[vmem, vmem, vmem],
        out_specs=hbm,
        scratch_shapes=[pltpu.VMEM((pix, ch), F32), dma],
    )(mine, left, right)


def solution(mesh):
    placed = (P("pix", "chan"), P(), P())
    return jax.shard_map(
        per_device, mesh=mesh, in_specs=placed, out_specs=P("pix", "chan"), check_vma=False
    )
```
